32 devices in a mesh: expert: 16 (over z, y, x), tensor: 2 (over core).
Axes of the slice: x: 2, y: 2, z: 4, core: 2. Of those that a mesh axis runs over, the one named last changes fastest.
Arguments:
- block_in: bfloat16 [8192, 1536], P('expert'), may hold values from -6 to 6
- segments: int32 [8192], P('expert'), may hold values from 0 to 31, never falling along the last dimension, each value on 1 to 1024 neighbouring positions
- routes: int32 [8192, 8], P('expert'), may hold values from 0 to 15, all different within a row; in each aligned block of 512 rows (0 to 511, 512 to 1023, ...) at most 320 rows name the same one
- route_weights: float32 [8192, 8], P('expert'), may hold values from 0.05 to 0.25
- gain_attn: float32 [1536], replicated, may hold values from 0.5 to 1.5
- gain_ffn: float32 [1536], replicated, may hold values from 0.5 to 1.5
- w_query: bfloat16 [1536, 1536], P(None, 'tensor'), may hold values from -0.15625 to 0.15625
- w_key: bfloat16 [1536, 512], P(None, 'tensor'), may hold values from -0.15625 to 0.15625
- w_value: bfloat16 [1536, 512], P(None, 'tensor'), may hold values from -0.15625 to 0.15625
- w_out_proj: bfloat16 [1536, 1536], P('tensor'), may hold values from -0.625 to 0.625
- w_gate: bfloat16 [16, 1536, 512], P('expert', None, 'tensor'), may hold values from -0.15625 to 0.15625
- w_up: bfloat16 [16, 1536, 512], P('expert', None, 'tensor'), may hold values from -0.15625 to 0.15625
- w_down: bfloat16 [16, 512, 1536], P('expert', 'tensor'), may hold values from -0.75 to 0.75
- mom_query: float32 [1536, 1536], P(None, 'tensor'), may hold values from -24 to 24
- mom_key: float32 [1536, 512], P(None, 'tensor'), may hold values from -24 to 24
- mom_value: float32 [1536, 512], P(None, 'tensor'), may hold values from -640 to 640
- mom_out_proj: float32 [1536, 1536], P('tensor'), may hold values from -24 to 24
- mom_gate: float32 [16, 1536, 512], P('expert', None, 'tensor'), may hold values from -6 to 6
- mom_up: float32 [16, 1536, 512], P('expert', None, 'tensor'), may hold values from -6 to 6
- mom_down: float32 [16, 512, 1536], P('expert', 'tensor'), may hold values from -6 to 6
- mom_gain_attn: float32 [1536], replicated, may hold values from -256 to 256
- mom_gain_ffn: float32 [1536], replicated, may hold values from -256 to 256
- cotangent: bfloat16 [8192, 1536], P('expert'), may hold values from -6 to 6
Outputs:
- block_out: bfloat16 [8192, 1536], P('expert')
- grad_input: float32 [8192, 1536], P('expert')
- grad_query: float32 [1536, 1536], P(None, 'tensor')
- grad_key: float32 [1536, 512], P(None, 'tensor')
- grad_value: float32 [1536, 512], P(None, 'tensor')
- grad_out_proj: float32 [1536, 1536], P('tensor')
- grad_gate: float32 [16, 1536, 512], P('expert', None, 'tensor')
- grad_up: float32 [16, 1536, 512], P('expert', None, 'tensor')
- grad_down: float32 [16, 512, 1536], P('expert', 'tensor')
- grad_gain_attn: float32 [1536], replicated
- grad_gain_ffn: float32 [1536], replicated
- new_query: float32 [1536, 1536], P('expert', 'tensor')
- new_key: float32 [1536, 512], P('expert', 'tensor')
- new_value: float32 [1536, 512], P('expert', 'tensor')
- new_out_proj: float32 [1536, 1536], P('tensor', 'expert')
- new_gate: float32 [16, 1536, 512], P('expert', None, 'tensor')
- new_up: float32 [16, 1536, 512], P('expert', None, 'tensor')
- new_down: float32 [16, 512, 1536], P('expert', 'tensor')
- new_gain_attn: float32 [1536], replicated
- new_gain_ffn: float32 [1536], replicated
- new_mom_query: float32 [1536, 1536], P(None, 'tensor')
- new_mom_key: float32 [1536, 512], P(None, 'tensor')
- new_mom_value: float32 [1536, 512], P(None, 'tensor')
- new_mom_out_proj: float32 [1536, 1536], P('tensor')
- new_mom_gate: float32 [16, 1536, 512], P('expert', None, 'tensor')
- new_mom_up: float32 [16, 1536, 512], P('expert', None, 'tensor')
- new_mom_down: float32 [16, 512, 1536], P('expert', 'tensor')
- new_mom_gain_attn: float32 [1536], replicated
- new_mom_gain_ffn: float32 [1536], replicated
The draws below stay inside these ranges and needn't reach their ends.
Inputs may be any that keep to these rules, and one draw needn't show every extreme that they name: `routes`: each row names 8 different experts; among the rows of one index of expert no expert is named more than 320 times.
All inputs are finite; a program needn't handle non-finite values.
Results may differ from the reference program's by a relative error of at most 0.025.
Values may be sent and summed in bfloat16 or wider, within the bound.
No kernel may reach another device: no remote copies, remote signals or barrier semaphores. Data moves between devices by JAX's collectives and lax.ppermute only.
A program may use at most 384 MiB of HBM per device.

```python
import math
import jax
import jax.numpy as jnp
import numpy as np
from jax import lax

D = 1536
HEADS = 24
KV = 8
HD = 64
FF = 512
TOPK = 8
SEQ = 512
NS_ITERS = 3
TOK_DEV = 512
EXPERTS = 16
TOKENS = 8192
CAP = 320
N_EXPERT = 16
N_TENSOR = 2


def steps_of(own_key, extent, shards, low, largest):
    factor_of = 1.0
    for axis_at, blocks in shards:
        draws = jax.random.uniform(jax.random.fold_in(jax.random.fold_in(own_key, 6), axis_at), (blocks,), jnp.float32, low / len(shards), largest / len(shards))
        factor_of = factor_of * jnp.repeat(jnp.exp(draws), extent[axis_at] // blocks).reshape((-1,) + (1,) * (len(extent) - 1 - axis_at))
    return factor_of


def split_up(number_of, total, most, slope):
    loads = [(1 << 20) // math.isqrt(grade ** slope) + 1 for grade in range(2, number_of + 1)]
    surplus, given = total - most - (number_of - 1), [1] * (number_of - 1)
    while surplus > 0:
        candidates = [i for i in range(number_of - 1) if given[i] < most]
        pool, budget = sum([loads[i] for i in candidates]), surplus
        for i in candidates:
            addition = min(most - given[i], max(1, budget * loads[i] // pool), surplus)
            given[i] = given[i] + addition
            surplus = surplus - addition
    return np.array([most] + given)


def ragged(stream_key, number_of, total, most, skew):
    if number_of == 2:
        one = jax.random.randint(stream_key, (), max(1, total - most), min(most, total - 1) + 1)
        return jnp.stack([one, total - one])
    tallies = jnp.asarray(split_up(number_of, total, most, skew), jnp.int32)
    couples = (number_of - 1) // 2
    source_of, taker = tallies[1:1 + 2 * couples:2], tallies[2:2 + 2 * couples:2]
    margin = jnp.minimum(source_of - 1, most - taker)
    passed = jax.random.randint(jax.random.fold_in(stream_key, 1), (couples,), 0, 1 << 20) % (margin + 1)
    tallies = tallies.at[1:1 + 2 * couples:2].set(source_of - passed).at[2:2 + 2 * couples:2].set(taker + passed)
    return tallies[jax.random.permutation(jax.random.fold_in(stream_key, 2), number_of)]


def routed_block(rng, own, number, rows, amount, top, reach, slope):
    order = jax.random.permutation(rng, amount)
    heavy_load, usual = shares(amount, rows * top, reach, slope, True), shares(amount, rows * top, reach, slope, False)
    places = jnp.arange(amount)

    def named(sizes, turn):
        used = int((sizes > 0).sum())
        fixed = max(1, used // 4)
        passed = fixed + (places - fixed + turn * (used - fixed)) % max(1, amount - fixed)
        return jnp.zeros((amount,), jnp.int32).at[order[jnp.where(places < fixed, places, passed)]].set(jnp.asarray(sizes, jnp.int32))

    sizes = jnp.where(number % 4 == 0, named(heavy_load, number // 4), named(usual, number - number // 4 - 1))
    mixed = jax.random.permutation(jax.random.fold_in(own, 3), amount)
    donor, receiver = mixed[0:amount // 2 * 2:2], mixed[1:amount // 2 * 2:2]
    margin = jnp.minimum(sizes[donor] - 1, reach - sizes[receiver]) // 2
    margin = jnp.where((donor == order[0]) | (receiver == order[0]) | (sizes[receiver] == 0), 0, jnp.maximum(margin, 0))
    passed = jax.random.randint(jax.random.fold_in(own, 4), (amount // 2,), 0, 1 << 20) % (margin + 1)
    sizes = sizes.at[donor].add(-passed).at[receiver].add(passed)
    members = jnp.searchsorted(jnp.cumsum(sizes), jnp.arange(rows * top), side="right").astype(jnp.int32)
    grid = members.reshape(top, rows).T
    grid = grid[jax.random.permutation(jax.random.fold_in(own, 1), rows)]
    turn = jax.random.randint(jax.random.fold_in(own, 2), (rows, 1), 0, top)
    return jnp.take_along_axis(grid, (jnp.arange(top)[None, :] + turn) % top, axis=1)


def shares(number_of, total, most, lean, full):
    portions = [(1 << 20) // math.isqrt(rank ** lean) + 1 for rank in range(1, number_of + 1)]
    largest = most if full else min(most, max(-(-total // number_of), total * portions[0] // sum(portions)))
    least = 1 if total - largest >= number_of - 1 else 0
    given, rest = [largest] + [least] * (number_of - 1), total - largest - least * (number_of - 1)
    while rest > 0:
        movable = [i for i in range(1, number_of) if given[i] < largest] or [i for i in range(1, number_of) if given[i] < most]
        mass, budget = sum([portions[i] for i in movable]), rest
        for i in movable:
            extra = min(most - given[i], max(1, budget * portions[i] // mass), rest)
            given[i] = given[i] + extra
            rest = rest - extra
    return np.array(given)


def gaussian(rng, shape, spread, most, shards=(), kind=jnp.bfloat16):
    loudness = steps_of(rng, shape, shards, -0.22, 0.18) if shards else 1.0
    array = jax.random.normal(rng, shape, jnp.float32) * spread * loudness
    return jnp.minimum(jnp.maximum(array, -most), most).astype(kind)


def setup_inputs(seed: int = 0) -> dict:
    splits = jax.random.split(jax.random.key(seed), 24)
    block_in = gaussian(splits[0], (TOKENS, D), 1.0, 6.0, ((0, 16),))
    segments = jnp.searchsorted(jnp.cumsum(ragged(splits[1], TOKENS // 256, TOKENS, min(1024, TOKENS // 2), 1)), jnp.arange(TOKENS), side="right").astype(jnp.int32)
    routes_keys = jax.random.split(jax.random.fold_in(splits[2], 1), TOKENS // TOK_DEV)
    routes_turns = jax.random.permutation(jax.random.fold_in(splits[2], 3), TOKENS // TOK_DEV)
    routes = jax.vmap(lambda own, number: routed_block(jax.random.fold_in(splits[2], 2), own, number, TOK_DEV, EXPERTS, TOPK, CAP, 1))(routes_keys, routes_turns).reshape((TOKENS, TOPK))
    route_weights = jnp.clip(0.05 + 0.2 * jax.random.uniform(splits[3], (TOKENS, TOPK), jnp.float32) ** steps_of(splits[3], (TOKENS, TOPK), ((0, 16),), -0.2, 0.2), 0.05, 0.25)
    gain_attn = jnp.clip(1.0 + 0.1 * jax.random.normal(splits[4], (D,), jnp.float32), 0.5, 1.5)
    gain_ffn = jnp.clip(1.0 + 0.1 * jax.random.normal(splits[5], (D,), jnp.float32), 0.5, 1.5)
    w_query = gaussian(splits[6], (D, HEADS * HD), D ** -0.5, 0.15625, ((1, 2),))
    w_key = gaussian(splits[7], (D, KV * HD), D ** -0.5, 0.15625, ((1, 2),))
    w_value = gaussian(splits[8], (D, KV * HD), D ** -0.5, 0.15625, ((1, 2),))
    w_out_proj = gaussian(splits[9], (HEADS * HD, D), (HEADS * HD // 16) ** -0.5, 0.625, ((0, 2),))
    w_gate = gaussian(splits[10], (EXPERTS, D, FF), D ** -0.5, 0.15625, ((0, 16), (2, 2)))
    w_up = gaussian(splits[11], (EXPERTS, D, FF), D ** -0.5, 0.15625, ((0, 16), (2, 2)))
    w_down = gaussian(splits[12], (EXPERTS, FF, D), (FF // 8) ** -0.5, 0.75, ((0, 16), (1, 2)))
    mom_query = gaussian(splits[13], (D, HEADS * HD), 4.0, 24.0, ((1, 2),), jnp.float32)
    mom_key = gaussian(splits[14], (D, KV * HD), 4.0, 24.0, ((1, 2),), jnp.float32)
    mom_value = gaussian(splits[15], (D, KV * HD), 100.0, 640.0, ((1, 2),), jnp.float32)
    mom_out_proj = gaussian(splits[16], (HEADS * HD, D), 4.0, 24.0, ((0, 2),), jnp.float32)
    mom_gate = gaussian(splits[17], (EXPERTS, D, FF), 1.0, 6.0, ((0, 16), (2, 2)), jnp.float32)
    mom_up = gaussian(splits[18], (EXPERTS, D, FF), 1.0, 6.0, ((0, 16), (2, 2)), jnp.float32)
    mom_down = gaussian(splits[19], (EXPERTS, FF, D), 1.0, 6.0, ((0, 16), (1, 2)), jnp.float32)
    mom_gain_attn = gaussian(splits[20], (D,), 40.0, 256.0, (), jnp.float32)
    mom_gain_ffn = gaussian(splits[21], (D,), 40.0, 256.0, (), jnp.float32)
    cotangent = gaussian(splits[22], (TOKENS, D), 1.0, 6.0, ((0, 16),))
    return dict(block_in=block_in, segments=segments, routes=routes, route_weights=route_weights, gain_attn=gain_attn, gain_ffn=gain_ffn, w_query=w_query, w_key=w_key, w_value=w_value, w_out_proj=w_out_proj, w_gate=w_gate, w_up=w_up, w_down=w_down, mom_query=mom_query, mom_key=mom_key, mom_value=mom_value, mom_out_proj=mom_out_proj, mom_gate=mom_gate, mom_up=mom_up, mom_down=mom_down, mom_gain_attn=mom_gain_attn, mom_gain_ffn=mom_gain_ffn, cotangent=cotangent)


momentum_decay = 0.95
learn_rate = 0.2
gain_rate = 0.002
norm_eps = 1e-05
coeff_one = 3.4445
coeff_two = -4.775
coeff_three = 2.0315

def silu_grad(values):
    logistic = jax.nn.sigmoid(values)
    return logistic * (1.0 + values * (1.0 - logistic))

def causal_mask(seg_ids):
    length = seg_ids.shape[0]
    row_pos = lax.broadcasted_iota(jnp.int32, (length, length), 0)
    col_pos = lax.broadcasted_iota(jnp.int32, (length, length), 1)
    return (col_pos <= row_pos) & (seg_ids[:, None] == seg_ids[None, :])

def group_scores(queries, key_rows, mask):
    length = queries.shape[0]
    groups = key_rows.shape[1] // HD
    query_heads = queries.astype(jnp.float32).reshape(length, groups, -1, HD)
    key_heads = key_rows.astype(jnp.float32).reshape(length, groups, HD)
    scores = jnp.einsum('skgd,tkd->kgst', query_heads, key_heads)
    return jnp.where(mask[None, None], scores, -jnp.inf)

def attend_forward(bundle):
    queries, key_rows, value_rows, seg_ids = bundle
    length = queries.shape[0]
    groups = key_rows.shape[1] // HD
    scores = group_scores(queries, key_rows, causal_mask(seg_ids))
    highest = lax.optimization_barrier(jnp.max(scores, axis=3, keepdims=True))
    log_total = highest + jnp.log(lax.optimization_barrier(jnp.sum(jnp.exp(scores - highest), axis=3, keepdims=True)))
    attn_probs = jnp.exp(scores - log_total).astype(jnp.bfloat16)
    value_heads = value_rows.astype(jnp.float32).reshape(length, groups, HD)
    attn_mixed = jnp.einsum('kgst,tkd->skgd', attn_probs.astype(jnp.float32), value_heads)
    return (log_total, attn_mixed.reshape(length, -1).astype(jnp.bfloat16))

def attend_backward(bundle):
    queries, key_rows, value_rows, seg_ids, log_total, attn_mixed, grad_mixed = bundle
    length = queries.shape[0]
    groups = key_rows.shape[1] // HD
    scores = group_scores(queries, key_rows, causal_mask(seg_ids))
    probs_full = jnp.exp(scores - log_total)
    attn_probs = probs_full.astype(jnp.bfloat16)
    grad_heads = grad_mixed.astype(jnp.float32).reshape(length, groups, -1, HD)
    value_heads = value_rows.astype(jnp.float32).reshape(length, groups, HD)
    grad_probs = jnp.einsum('skgd,tkd->kgst', grad_heads, value_heads)
    offset = jnp.einsum('skgd,skgd->kgs', grad_heads, attn_mixed.astype(jnp.float32).reshape(length, groups, -1, HD))
    grad_scores = (probs_full * (grad_probs - offset[..., None])).astype(jnp.bfloat16).astype(jnp.float32)
    key_heads = key_rows.astype(jnp.float32).reshape(length, groups, HD)
    query_heads = queries.astype(jnp.float32).reshape(length, groups, -1, HD)
    grad_queries = (jnp.einsum('kgst,tkd->skgd', grad_scores, key_heads) * HD ** (-0.5)).reshape(length, -1).astype(jnp.bfloat16)
    grad_keys = jnp.einsum('kgst,skgd->tkd', grad_scores, query_heads).reshape(length, -1).astype(jnp.bfloat16)
    grad_values = jnp.einsum('kgst,skgd->tkd', attn_probs.astype(jnp.float32), grad_heads).reshape(length, -1).astype(jnp.bfloat16)
    return (grad_queries, grad_keys, grad_values)

def newton_schulz(matrix):
    flipped = matrix.shape[0] > matrix.shape[1]
    oriented = matrix.T if flipped else matrix
    frob_norm = jnp.sqrt(jnp.sum(oriented * oriented)) + 1e-07
    iterate = (oriented / frob_norm).astype(jnp.bfloat16)
    for sweep_index in range(NS_ITERS):
        gram_mat = jnp.dot(iterate, iterate.T, preferred_element_type=jnp.float32).astype(jnp.bfloat16)
        square = jnp.dot(gram_mat, gram_mat, preferred_element_type=jnp.float32)
        poly_mix = (coeff_two * gram_mat.astype(jnp.float32) + coeff_three * square).astype(jnp.bfloat16)
        iterate = (coeff_one * iterate.astype(jnp.float32) + jnp.dot(poly_mix, iterate, preferred_element_type=jnp.float32)).astype(jnp.bfloat16)
    return iterate.T if flipped else iterate

def muon_matrix(bundle):
    weight, moment, gradient = bundle
    new_moment = momentum_decay * moment + gradient
    ortho_piece = newton_schulz(new_moment)
    factor = learn_rate * 0.2 * math.sqrt(max(weight.shape[-2], weight.shape[-1]))
    return (weight.astype(jnp.float32) - factor * ortho_piece.astype(jnp.float32), new_moment)

def reference(block_in, segments, routes, route_weights, gain_attn, gain_ffn, w_query, w_key, w_value, w_out_proj, w_gate, w_up, w_down, mom_query, mom_key, mom_value, mom_out_proj, mom_gate, mom_up, mom_down, mom_gain_attn, mom_gain_ffn, cotangent):
    seq_total = TOKENS // SEQ
    residual_in = block_in.astype(jnp.float32)
    grad_top = cotangent.astype(jnp.float32)

    def first_half(seq_rows, seg_ids):
        inv_first = lax.rsqrt(lax.optimization_barrier(jnp.mean(seq_rows * seq_rows, axis=1, keepdims=True)) + norm_eps)
        normed_attn = (seq_rows * inv_first * gain_attn).astype(jnp.bfloat16)
        queries = (jnp.dot(normed_attn, w_query, preferred_element_type=jnp.float32) * HD ** (-0.5)).astype(jnp.bfloat16)
        key_rows = jnp.dot(normed_attn, w_key, preferred_element_type=jnp.float32).astype(jnp.bfloat16)
        value_rows = jnp.dot(normed_attn, w_value, preferred_element_type=jnp.float32).astype(jnp.bfloat16)
        log_total, attn_mixed = attend_forward((queries, key_rows, value_rows, seg_ids))
        return (inv_first, normed_attn, queries, key_rows, value_rows, log_total, attn_mixed)

    def forward_seq(bundle):
        seq_rows, seg_ids = bundle
        pieces = first_half(seq_rows, seg_ids)
        return seq_rows + jnp.dot(pieces[6], w_out_proj, preferred_element_type=jnp.float32)
    seq_inputs = residual_in.reshape(seq_total, SEQ, D)
    seg_inputs = segments.reshape(seq_total, SEQ)
    hidden_state = lax.map(forward_seq, (seq_inputs, seg_inputs)).reshape(TOKENS, D)
    inv_second = lax.rsqrt(lax.optimization_barrier(jnp.mean(hidden_state * hidden_state, axis=1, keepdims=True)) + norm_eps)
    normed_ffn = (hidden_state * inv_second * gain_ffn).astype(jnp.bfloat16)
    limit = N_EXPERT * CAP
    dummy = TOKENS * TOPK
    quarter = FF // N_TENSOR
    flat_routes = routes.reshape(-1)
    pad_weights = jnp.concatenate([route_weights.reshape(-1), jnp.zeros((1,), jnp.float32)])
    pad_rows = jnp.concatenate([normed_ffn, jnp.zeros((1, D), jnp.bfloat16)])
    pad_grad = jnp.concatenate([grad_top, jnp.zeros((1, D), jnp.float32)])

    def expert_step(carry, bundle):
        moe_sum, grad_sum = carry
        expert_id, gate_mat, up_mat, down_mat = bundle
        picked = jnp.nonzero(flat_routes == expert_id, size=limit, fill_value=dummy)[0].astype(jnp.int32)
        token_ids = picked // TOPK
        scale_rows = pad_weights[picked][:, None]
        rows_in = pad_rows[token_ids]
        gate_act = jnp.dot(rows_in, gate_mat, preferred_element_type=jnp.float32)
        up_act = jnp.dot(rows_in, up_mat, preferred_element_type=jnp.float32)
        activated = jax.nn.silu(gate_act)
        hidden = (activated * up_act).astype(jnp.bfloat16)
        grad_rows = (scale_rows * pad_grad[token_ids]).astype(jnp.bfloat16)
        grad_hidden = jnp.dot(grad_rows, down_mat.T, preferred_element_type=jnp.float32)
        grad_gate_act = (grad_hidden * up_act * silu_grad(gate_act)).astype(jnp.bfloat16)
        grad_up_act = (grad_hidden * activated).astype(jnp.bfloat16)
        grad_down_mat = jnp.dot(hidden.T, grad_rows, preferred_element_type=jnp.float32)
        grad_gate_mat = jnp.dot(rows_in.T, grad_gate_act, preferred_element_type=jnp.float32)
        grad_up_mat = jnp.dot(rows_in.T, grad_up_act, preferred_element_type=jnp.float32)
        out_total = jnp.zeros((limit, D), jnp.float32)
        input_total = jnp.zeros((limit, D), jnp.float32)
        for part_index in range(N_TENSOR):
            low_edge = part_index * quarter
            high_edge = low_edge + quarter
            expert_part = jnp.dot(hidden[:, low_edge:high_edge], down_mat[low_edge:high_edge], preferred_element_type=jnp.float32).astype(jnp.bfloat16)
            out_total = out_total + lax.optimization_barrier(expert_part).astype(jnp.float32)
            input_part = jnp.dot(grad_gate_act[:, low_edge:high_edge], gate_mat[:, low_edge:high_edge].T, preferred_element_type=jnp.float32)
            input_part = input_part + jnp.dot(grad_up_act[:, low_edge:high_edge], up_mat[:, low_edge:high_edge].T, preferred_element_type=jnp.float32)
            input_total = input_total + lax.optimization_barrier(input_part.astype(jnp.bfloat16)).astype(jnp.float32)
        moe_sum = moe_sum.at[token_ids].add(scale_rows * out_total)
        grad_sum = grad_sum.at[token_ids].add(input_total)
        return ((moe_sum, grad_sum), (grad_gate_mat, grad_up_mat, grad_down_mat))
    start_sums = (jnp.zeros((TOKENS + 1, D), jnp.float32), jnp.zeros((TOKENS + 1, D), jnp.float32))
    expert_ids = jnp.arange(EXPERTS, dtype=jnp.int32)
    (moe_sum, grad_sum), (grad_gate, grad_up, grad_down) = lax.scan(expert_step, start_sums, (expert_ids, w_gate, w_up, w_down))
    block_out = (hidden_state + moe_sum[:TOKENS]).astype(jnp.bfloat16)
    grad_normed_ffn = grad_sum[:TOKENS]

    def backward_seq(carry, bundle):
        seq_rows, seg_ids, state_rows, grad_ffn_rows, top_rows = bundle
        inv_first, normed_attn, queries, key_rows, value_rows, log_total, attn_mixed = first_half(seq_rows, seg_ids)
        inv_state = lax.rsqrt(lax.optimization_barrier(jnp.mean(state_rows * state_rows, axis=1, keepdims=True)) + norm_eps)
        gain_ffn_part = lax.optimization_barrier(jnp.sum(grad_ffn_rows * state_rows * inv_state, axis=0))
        scaled = grad_ffn_rows * gain_ffn
        grad_state = top_rows + inv_state * (scaled - state_rows * inv_state * inv_state * lax.optimization_barrier(jnp.mean(scaled * state_rows, axis=1, keepdims=True)))
        grad_state_low = grad_state.astype(jnp.bfloat16)
        grad_out_mat = jnp.dot(attn_mixed.T, grad_state_low, preferred_element_type=jnp.float32)
        grad_mixed = jnp.dot(grad_state_low, w_out_proj.T, preferred_element_type=jnp.float32).astype(jnp.bfloat16)
        grad_queries, grad_keys, grad_values = attend_backward((queries, key_rows, value_rows, seg_ids, log_total, attn_mixed, grad_mixed))
        grad_query_mat = jnp.dot(normed_attn.T, grad_queries, preferred_element_type=jnp.float32)
        grad_key_mat = jnp.dot(normed_attn.T, grad_keys, preferred_element_type=jnp.float32)
        grad_value_mat = jnp.dot(normed_attn.T, grad_values, preferred_element_type=jnp.float32)
        grad_normed_attn = jnp.dot(grad_queries, w_query.T, preferred_element_type=jnp.float32)
        grad_normed_attn = grad_normed_attn + jnp.dot(grad_keys, w_key.T, preferred_element_type=jnp.float32)
        grad_normed_attn = grad_normed_attn + jnp.dot(grad_values, w_value.T, preferred_element_type=jnp.float32)
        gain_attn_part = lax.optimization_barrier(jnp.sum(grad_normed_attn * seq_rows * inv_first, axis=0))
        scaled_first = grad_normed_attn * gain_attn
        grad_rows_in = grad_state + inv_first * (scaled_first - seq_rows * inv_first * inv_first * lax.optimization_barrier(jnp.mean(scaled_first * seq_rows, axis=1, keepdims=True)))
        terms = (grad_query_mat, grad_key_mat, grad_value_mat, grad_out_mat, gain_attn_part, gain_ffn_part)
        return (jax.tree.map(jnp.add, carry, terms), grad_rows_in)
    start_grads = (jnp.zeros(w_query.shape, jnp.float32), jnp.zeros(w_key.shape, jnp.float32), jnp.zeros(w_value.shape, jnp.float32), jnp.zeros(w_out_proj.shape, jnp.float32), jnp.zeros((D,), jnp.float32), jnp.zeros((D,), jnp.float32))
    back_inputs = (seq_inputs, seg_inputs, hidden_state.reshape(seq_total, SEQ, D), grad_normed_ffn.reshape(seq_total, SEQ, D), grad_top.reshape(seq_total, SEQ, D))
    sums, grad_seqs = lax.scan(backward_seq, start_grads, back_inputs)
    grad_query, grad_key, grad_value, grad_out_proj, grad_gain_attn, grad_gain_ffn = sums
    grad_input = grad_seqs.reshape(TOKENS, D)
    new_query, new_mom_query = muon_matrix((w_query, mom_query, grad_query))
    new_key, new_mom_key = muon_matrix((w_key, mom_key, grad_key))
    new_value, new_mom_value = muon_matrix((w_value, mom_value, grad_value))
    new_out_proj, new_mom_out_proj = muon_matrix((w_out_proj, mom_out_proj, grad_out_proj))
    new_gate, new_mom_gate = lax.map(muon_matrix, (w_gate, mom_gate, grad_gate))
    new_up, new_mom_up = lax.map(muon_matrix, (w_up, mom_up, grad_up))
    new_down, new_mom_down = lax.map(muon_matrix, (w_down, mom_down, grad_down))
    new_mom_gain_attn = momentum_decay * mom_gain_attn + grad_gain_attn
    new_mom_gain_ffn = momentum_decay * mom_gain_ffn + grad_gain_ffn
    new_gain_attn = gain_attn - gain_rate * new_mom_gain_attn
    new_gain_ffn = gain_ffn - gain_rate * new_mom_gain_ffn
    return (block_out, grad_input, grad_query, grad_key, grad_value, grad_out_proj, grad_gate, grad_up, grad_down, grad_gain_attn, grad_gain_ffn, new_query, new_key, new_value, new_out_proj, new_gate, new_up, new_down, new_gain_attn, new_gain_ffn, new_mom_query, new_mom_key, new_mom_value, new_mom_out_proj, new_mom_gate, new_mom_up, new_mom_down, new_mom_gain_attn, new_mom_gain_ffn)
```

```python
import math

import jax
import jax.numpy as jnp
from jax import lax
from jax.experimental import pallas as pl
from jax.experimental.pallas import tpu as pltpu
from jax.sharding import PartitionSpec as P

HD = 64
TOPK = 8
SEQ = 512
NS_ITERS = 3


momentum_decay = 0.95
learn_rate = 0.2
gain_rate = 0.002
norm_eps = 1e-05
coeff_one = 3.4445
coeff_two = -4.775
coeff_three = 2.0315


def shortened(value):

    def short(part):
        return part.astype(jnp.bfloat16) if part.dtype == jnp.float32 else part

    return jax.tree.map(short, value)


def spread(value, axis, root):
    mine = lax.axis_index(axis) == root
    return lax.psum(jnp.where(mine, value, jnp.zeros_like(value)), axis)


def silu_grad(values):
    logistic = jax.nn.sigmoid(values)
    return logistic * (1.0 + values * (1.0 - logistic))


def causal_mask(seg_ids):
    length = seg_ids.shape[0]
    row_pos = lax.broadcasted_iota(jnp.int32, (length, length), 0)
    col_pos = lax.broadcasted_iota(jnp.int32, (length, length), 1)
    return (col_pos <= row_pos) & (seg_ids[:, None] == seg_ids[None, :])


def group_scores(queries, key_rows, mask):
    length = queries.shape[0]
    groups = key_rows.shape[1] // HD
    query_heads = queries.reshape(length, groups, -1, HD)
    key_heads = key_rows.reshape(length, groups, HD)
    scores = jnp.einsum(
        "skgd,tkd->kgst", query_heads, key_heads, preferred_element_type=jnp.float32
    )
    return jnp.where(mask[None, None], scores, -jnp.inf)


def attend_forward(bundle):
    queries, key_rows, value_rows, seg_ids = bundle
    length = queries.shape[0]
    groups = key_rows.shape[1] // HD
    scores = group_scores(queries, key_rows, causal_mask(seg_ids))
    highest = jnp.max(scores, axis=3, keepdims=True)
    log_total = highest + jnp.log(jnp.sum(jnp.exp(scores - highest), axis=3, keepdims=True))
    attn_probs = jnp.exp(scores - log_total).astype(jnp.bfloat16)
    attn_mixed = jnp.einsum(
        "kgst,tkd->skgd",
        attn_probs,
        value_rows.reshape(length, groups, HD),
        preferred_element_type=jnp.float32,
    )
    return (log_total, attn_mixed.reshape(length, -1).astype(jnp.bfloat16))


def attend_backward(bundle):
    queries, key_rows, value_rows, seg_ids, log_total, attn_mixed, grad_mixed = bundle
    length = queries.shape[0]
    groups = key_rows.shape[1] // HD
    scores = group_scores(queries, key_rows, causal_mask(seg_ids))
    probs_full = jnp.exp(scores - log_total)
    attn_probs = probs_full.astype(jnp.bfloat16)
    grad_heads = grad_mixed.reshape(length, groups, -1, HD)
    grad_probs = jnp.einsum(
        "skgd,tkd->kgst",
        grad_heads,
        value_rows.reshape(length, groups, HD),
        preferred_element_type=jnp.float32,
    )
    offset = jnp.einsum(
        "skgd,skgd->kgs",
        grad_heads,
        attn_mixed.reshape(length, groups, -1, HD),
        preferred_element_type=jnp.float32,
    )
    grad_scores = (probs_full * (grad_probs - offset[..., None])).astype(jnp.bfloat16)
    grad_queries = jnp.einsum(
        "kgst,tkd->skgd",
        grad_scores,
        key_rows.reshape(length, groups, HD),
        preferred_element_type=jnp.float32,
    )
    grad_queries = (grad_queries * HD ** (-0.5)).reshape(length, -1).astype(jnp.bfloat16)
    grad_keys = jnp.einsum(
        "kgst,skgd->tkd",
        grad_scores,
        queries.reshape(length, groups, -1, HD),
        preferred_element_type=jnp.float32,
    )
    grad_values = jnp.einsum(
        "kgst,skgd->tkd", attn_probs, grad_heads, preferred_element_type=jnp.float32
    )
    return (
        grad_queries,
        grad_keys.reshape(length, -1).astype(jnp.bfloat16),
        grad_values.reshape(length, -1).astype(jnp.bfloat16),
    )


def newton_schulz(matrix):
    flipped = matrix.shape[0] > matrix.shape[1]
    oriented = matrix.T if flipped else matrix
    frob_norm = jnp.sqrt(jnp.sum(oriented * oriented)) + 1e-07
    iterate = (oriented / frob_norm).astype(jnp.bfloat16)
    for sweep_index in range(NS_ITERS):
        gram_mat = jnp.dot(iterate, iterate.T, preferred_element_type=jnp.float32).astype(
            jnp.bfloat16
        )
        square = jnp.dot(gram_mat, gram_mat, preferred_element_type=jnp.float32)
        poly_mix = (coeff_two * gram_mat.astype(jnp.float32) + coeff_three * square).astype(
            jnp.bfloat16
        )
        iterate = (
            coeff_one * iterate.astype(jnp.float32)
            + jnp.dot(poly_mix, iterate, preferred_element_type=jnp.float32)
        ).astype(jnp.bfloat16)
    return iterate.T if flipped else iterate


def zero_ortho(matrix):
    return jnp.zeros(matrix.shape, jnp.bfloat16)


def solve_set(which_set):

    def solve_branch(matrices):
        return tuple(
            (
                (
                    newton_schulz(matrices[index])
                    if index in which_set
                    else zero_ortho(matrices[index])
                )
                for index in range(len(matrices))
            )
        )

    return solve_branch


def per_device(
    block_in,
    segments,
    routes,
    route_weights,
    gain_attn,
    gain_ffn,
    w_query,
    w_key,
    w_value,
    w_out_proj,
    w_gate,
    w_up,
    w_down,
    mom_query,
    mom_key,
    mom_value,
    mom_out_proj,
    mom_gate,
    mom_up,
    mom_down,
    mom_gain_attn,
    mom_gain_ffn,
    cotangent,
):
    tok_rows, width = block_in.shape
    seq_count = tok_rows // SEQ
    tensor_count = lax.axis_size("tensor")
    expert_count = lax.axis_size("expert")
    tensor_pos = lax.axis_index("tensor")
    expert_pos = lax.axis_index("expert")
    residual_in = block_in.astype(jnp.float32)
    inv_first = lax.rsqrt(jnp.mean(residual_in * residual_in, axis=1, keepdims=True) + norm_eps)
    normed_attn = (residual_in * inv_first * gain_attn).astype(jnp.bfloat16)
    queries = (
        jnp.dot(normed_attn, w_query, preferred_element_type=jnp.float32) * HD ** (-0.5)
    ).astype(jnp.bfloat16)
    key_rows = jnp.dot(normed_attn, w_key, preferred_element_type=jnp.float32).astype(jnp.bfloat16)
    value_rows = jnp.dot(normed_attn, w_value, preferred_element_type=jnp.float32).astype(
        jnp.bfloat16
    )
    seq_items = (
        queries.reshape(seq_count, SEQ, -1),
        key_rows.reshape(seq_count, SEQ, -1),
        value_rows.reshape(seq_count, SEQ, -1),
        segments.reshape(seq_count, SEQ),
    )
    log_total, attn_mixed = lax.map(attend_forward, seq_items)
    mixed_flat = attn_mixed.reshape(tok_rows, -1)
    attn_part = jnp.dot(mixed_flat, w_out_proj, preferred_element_type=jnp.float32)
    hidden_state = residual_in + lax.psum(attn_part.astype(jnp.bfloat16), "tensor").astype(
        jnp.float32
    )
    inv_second = lax.rsqrt(jnp.mean(hidden_state * hidden_state, axis=1, keepdims=True) + norm_eps)
    normed_ffn = (hidden_state * inv_second * gain_ffn).astype(jnp.bfloat16)
    capacity = min(tok_rows, 5 * tok_rows * TOPK // (4 * expert_count) // 8 * 8)
    quarter_cap = capacity // tensor_count
    flat_routes = routes.reshape(-1)
    flat_weights = route_weights.reshape(-1)
    one_hot = (flat_routes[:, None] == jnp.arange(expert_count, dtype=jnp.int32)[None, :]).astype(
        jnp.int32
    )
    route_rank = jnp.sum((jnp.cumsum(one_hot, axis=0) - one_hot) * one_hot, axis=1)
    slot_ids = flat_routes * capacity + route_rank
    local_rank = route_rank - tensor_pos * quarter_cap
    inside = (local_rank >= 0) & (local_rank < quarter_cap)
    quarter_ids = flat_routes * quarter_cap + jnp.clip(local_rank, 0, quarter_cap - 1)

    def place_rows(row_values):
        slot_table = jnp.zeros((expert_count * capacity, width), jnp.bfloat16)
        return slot_table.at[slot_ids].set(row_values).reshape(expert_count, capacity, width)

    grad_top = cotangent.astype(jnp.float32)
    grad_routed = (jnp.repeat(grad_top, TOPK, axis=0) * flat_weights[:, None]).astype(jnp.bfloat16)
    routed_rows = place_rows(jnp.repeat(normed_ffn, TOPK, axis=0))
    received = lax.all_to_all(routed_rows, "expert", split_axis=0, concat_axis=0, tiled=True)
    flat_rows = received.reshape(-1, width)
    gate_act = jnp.dot(flat_rows, w_gate[0], preferred_element_type=jnp.float32)
    up_act = jnp.dot(flat_rows, w_up[0], preferred_element_type=jnp.float32)
    hidden = (jax.nn.silu(gate_act) * up_act).astype(jnp.bfloat16)
    expert_part = jnp.dot(hidden, w_down[0], preferred_element_type=jnp.float32).astype(
        jnp.bfloat16
    )
    expert_out = expert_part.reshape(received.shape)
    summed = lax.psum_scatter(
        expert_out.astype(jnp.float32).astype(jnp.bfloat16),
        "tensor",
        scatter_dimension=1,
        tiled=True,
    ).astype(jnp.float32)
    returned = lax.all_to_all(
        summed.astype(jnp.bfloat16), "expert", split_axis=0, concat_axis=0, tiled=True
    ).astype(summed.dtype)
    picked = (
        returned.reshape(-1, width)[quarter_ids] * jnp.where(inside, flat_weights, 0.0)[:, None]
    )
    moe_part = jnp.sum(picked.reshape(tok_rows, TOPK, width), axis=1)
    block_out = (
        hidden_state + lax.psum(moe_part.astype(jnp.bfloat16), "tensor").astype(jnp.float32)
    ).astype(jnp.bfloat16)
    grad_received = lax.all_to_all(
        place_rows(grad_routed), "expert", split_axis=0, concat_axis=0, tiled=True
    )
    flat_rows = received.reshape(-1, width)
    flat_grad = grad_received.reshape(-1, width)
    gate_act = jnp.dot(flat_rows, w_gate[0], preferred_element_type=jnp.float32)
    up_act = jnp.dot(flat_rows, w_up[0], preferred_element_type=jnp.float32)
    activated = jax.nn.silu(gate_act)
    hidden = (activated * up_act).astype(jnp.bfloat16)
    grad_hidden = jnp.dot(flat_grad, w_down[0].T, preferred_element_type=jnp.float32)
    grad_gate_act = (grad_hidden * up_act * silu_grad(gate_act)).astype(jnp.bfloat16)
    grad_up_act = (grad_hidden * activated).astype(jnp.bfloat16)
    grad_down = jnp.dot(hidden.T, flat_grad, preferred_element_type=jnp.float32)[None]
    grad_gate = jnp.dot(flat_rows.T, grad_gate_act, preferred_element_type=jnp.float32)[None]
    grad_up = jnp.dot(flat_rows.T, grad_up_act, preferred_element_type=jnp.float32)[None]
    input_part = jnp.dot(grad_gate_act, w_gate[0].T, preferred_element_type=jnp.float32)
    input_part = input_part + jnp.dot(grad_up_act, w_up[0].T, preferred_element_type=jnp.float32)
    input_part = input_part.astype(jnp.bfloat16).reshape(expert_count, capacity, width)
    summed_grad = lax.psum_scatter(
        input_part.astype(jnp.float32).astype(jnp.bfloat16),
        "tensor",
        scatter_dimension=1,
        tiled=True,
    ).astype(jnp.float32)
    returned_grad = lax.all_to_all(
        summed_grad.astype(jnp.bfloat16), "expert", split_axis=0, concat_axis=0, tiled=True
    ).astype(summed_grad.dtype)
    picked_grad = (
        returned_grad.reshape(-1, width)[quarter_ids] * inside.astype(jnp.float32)[:, None]
    )
    ffn_part = jnp.sum(picked_grad.reshape(tok_rows, TOPK, width), axis=1)
    grad_normed_ffn = lax.psum(ffn_part.astype(jnp.bfloat16), "tensor").astype(jnp.float32)
    gain_ffn_part = jnp.sum(grad_normed_ffn * hidden_state * inv_second, axis=0)
    scaled = grad_normed_ffn * gain_ffn
    grad_state = grad_top + inv_second * (
        scaled
        - hidden_state
        * inv_second
        * inv_second
        * jnp.mean(scaled * hidden_state, axis=1, keepdims=True)
    )
    grad_state_low = grad_state.astype(jnp.bfloat16)
    grad_out_local = jnp.dot(mixed_flat.T, grad_state_low, preferred_element_type=jnp.float32)
    grad_mixed = jnp.dot(grad_state_low, w_out_proj.T, preferred_element_type=jnp.float32).astype(
        jnp.bfloat16
    )
    back_items = seq_items + (log_total, attn_mixed, grad_mixed.reshape(seq_count, SEQ, -1))
    grad_queries, grad_keys, grad_values = lax.map(attend_backward, back_items)
    grad_queries = grad_queries.reshape(tok_rows, -1)
    grad_keys = grad_keys.reshape(tok_rows, -1)
    grad_values = grad_values.reshape(tok_rows, -1)
    grad_query_local = jnp.dot(normed_attn.T, grad_queries, preferred_element_type=jnp.float32)
    grad_key_local = jnp.dot(normed_attn.T, grad_keys, preferred_element_type=jnp.float32)
    grad_value_local = jnp.dot(normed_attn.T, grad_values, preferred_element_type=jnp.float32)
    attn_input_part = jnp.dot(grad_queries, w_query.T, preferred_element_type=jnp.float32)
    attn_input_part = attn_input_part + jnp.dot(
        grad_keys, w_key.T, preferred_element_type=jnp.float32
    )
    attn_input_part = attn_input_part + jnp.dot(
        grad_values, w_value.T, preferred_element_type=jnp.float32
    )
    grad_normed_attn = lax.psum(attn_input_part.astype(jnp.bfloat16), "tensor").astype(jnp.float32)
    gain_attn_part = jnp.sum(grad_normed_attn * residual_in * inv_first, axis=0)
    scaled_first = grad_normed_attn * gain_attn
    grad_input = grad_state + inv_first * (
        scaled_first
        - residual_in
        * inv_first
        * inv_first
        * jnp.mean(scaled_first * residual_in, axis=1, keepdims=True)
    )
    grad_query, grad_key, grad_value, grad_out_proj, grad_gain_attn, grad_gain_ffn = (
        lax.psum(grad_query_local.astype(jnp.bfloat16), "expert").astype(jnp.float32),
        lax.psum(grad_key_local.astype(jnp.bfloat16), "expert").astype(jnp.float32),
        lax.psum(grad_value_local.astype(jnp.bfloat16), "expert").astype(jnp.float32),
        lax.psum(grad_out_local.astype(jnp.bfloat16), "expert").astype(jnp.float32),
        lax.psum(gain_attn_part.astype(jnp.bfloat16), "expert").astype(jnp.float32),
        lax.psum(gain_ffn_part.astype(jnp.bfloat16), "expert").astype(jnp.float32),
    )
    new_mom_query = momentum_decay * mom_query + grad_query
    new_mom_key = momentum_decay * mom_key + grad_key
    new_mom_value = momentum_decay * mom_value + grad_value
    new_mom_out_proj = momentum_decay * mom_out_proj + grad_out_proj
    new_mom_gate = momentum_decay * mom_gate + grad_gate
    new_mom_up = momentum_decay * mom_up + grad_up
    new_mom_down = momentum_decay * mom_down + grad_down
    new_mom_gain_attn = momentum_decay * mom_gain_attn + grad_gain_attn
    new_mom_gain_ffn = momentum_decay * mom_gain_ffn + grad_gain_ffn
    gathered = (
        lax.all_gather(new_mom_query.astype(jnp.bfloat16), "tensor", axis=1, tiled=True).astype(
            new_mom_query.dtype
        ),
        lax.all_gather(new_mom_key.astype(jnp.bfloat16), "tensor", axis=1, tiled=True).astype(
            new_mom_key.dtype
        ),
        lax.all_gather(new_mom_value.astype(jnp.bfloat16), "tensor", axis=1, tiled=True).astype(
            new_mom_value.dtype
        ),
        lax.all_gather(new_mom_out_proj.astype(jnp.bfloat16), "tensor", axis=0, tiled=True).astype(
            new_mom_out_proj.dtype
        ),
        lax.all_gather(new_mom_gate.astype(jnp.bfloat16), "tensor", axis=2, tiled=True).astype(
            new_mom_gate.dtype
        ),
        lax.all_gather(new_mom_up.astype(jnp.bfloat16), "tensor", axis=2, tiled=True).astype(
            new_mom_up.dtype
        ),
        lax.all_gather(new_mom_down.astype(jnp.bfloat16), "tensor", axis=1, tiled=True).astype(
            new_mom_down.dtype
        ),
    )

    def expert_rows(matrix, along_dim):
        row_width = matrix.shape[along_dim] // expert_count
        return lax.dynamic_slice_in_dim(matrix, expert_pos * row_width, row_width, along_dim)

    def apply_update(weight, ortho_piece, whole_shape):
        factor = learn_rate * 0.2 * math.sqrt(max(whole_shape[-2], whole_shape[-1]))
        return weight.astype(jnp.float32) - factor * ortho_piece.astype(jnp.float32)

    expert_branches = [
        solve_set(tuple((index for index in range(3) if index % tensor_count == position)))
        for position in range(tensor_count)
    ]
    ortho_gate, ortho_up, ortho_down = lax.switch(
        tensor_pos, expert_branches, (gathered[4][0], gathered[5][0], gathered[6][0])
    )
    piece_gate, piece_up, piece_down = (
        lax.psum_scatter(
            ortho_gate[None].astype(jnp.bfloat16), "tensor", scatter_dimension=2, tiled=True
        ).astype(jnp.float32),
        lax.psum_scatter(
            ortho_up[None].astype(jnp.bfloat16), "tensor", scatter_dimension=2, tiled=True
        ).astype(jnp.float32),
        lax.psum_scatter(
            ortho_down[None].astype(jnp.bfloat16), "tensor", scatter_dimension=1, tiled=True
        ).astype(jnp.float32),
    )
    new_gate = apply_update(w_gate, piece_gate, gathered[4].shape)
    new_up = apply_update(w_up, piece_up, gathered[5].shape)
    new_down = apply_update(w_down, piece_down, gathered[6].shape)
    owner_list = [index * expert_count // 4 for index in range(4)]
    which_owned = jnp.zeros((), jnp.int32)
    for index in range(4):
        which_owned = jnp.where(expert_pos == owner_list[index], index + 1, which_owned)
    attn_branches = [solve_set(())] + [solve_set((index,)) for index in range(4)]
    attn_orthos = lax.switch(
        which_owned, attn_branches, (gathered[0], gathered[1], gathered[2], gathered[3])
    )
    attn_list = (
        (1, w_query.shape[1]),
        (1, w_key.shape[1]),
        (1, w_value.shape[1]),
        (0, w_out_proj.shape[0]),
    )
    pieces = []
    for matrix_index in range(4):
        along_dim, piece_width = attn_list[matrix_index]
        pieces.append(
            spread(
                shortened(
                    lax.dynamic_slice_in_dim(
                        attn_orthos[matrix_index], tensor_pos * piece_width, piece_width, along_dim
                    )
                ),
                "expert",
                owner_list[matrix_index],
            )
        )
    new_query = apply_update(expert_rows(w_query, 0), expert_rows(pieces[0], 0), gathered[0].shape)
    new_key = apply_update(expert_rows(w_key, 0), expert_rows(pieces[1], 0), gathered[1].shape)
    new_value = apply_update(expert_rows(w_value, 0), expert_rows(pieces[2], 0), gathered[2].shape)
    new_out_proj = apply_update(
        expert_rows(w_out_proj, 1), expert_rows(pieces[3], 1), gathered[3].shape
    )
    new_gain_attn = gain_attn - gain_rate * new_mom_gain_attn
    new_gain_ffn = gain_ffn - gain_rate * new_mom_gain_ffn
    return (
        block_out,
        grad_input,
        grad_query,
        grad_key,
        grad_value,
        grad_out_proj,
        grad_gate,
        grad_up,
        grad_down,
        grad_gain_attn,
        grad_gain_ffn,
        new_query,
        new_key,
        new_value,
        new_out_proj,
        new_gate,
        new_up,
        new_down,
        new_gain_attn,
        new_gain_ffn,
        new_mom_query,
        new_mom_key,
        new_mom_value,
        new_mom_out_proj,
        new_mom_gate,
        new_mom_up,
        new_mom_down,
        new_mom_gain_attn,
        new_mom_gain_ffn,
    )


def chip_index(z, y, x):
    return (z * 2 + y) * 2 + x


def chip_pairs(target):
    return [
        (chip_index(z, y, x), chip_index(*target(z, y, x)))
        for z in range(4)
        for y in range(2)
        for x in range(2)
    ]


FLIP_X = chip_pairs(lambda z, y, x: (z, y, 1 - x))
FLIP_Y = chip_pairs(lambda z, y, x: (z, 1 - y, x))
FLIP_Z1 = chip_pairs(lambda z, y, x: (z ^ 1, y, x))
FLIP_Z2 = chip_pairs(lambda z, y, x: (z ^ 2, y, x))
TURN_UP = [chip_pairs(lambda z, y, x, k=k: ((z + k) % 4, y, x)) for k in range(4)]
TURN_DOWN = [chip_pairs(lambda z, y, x, k=k: ((z - k) % 4, y, x)) for k in range(4)]


def across(value, pairs):
    return lax.ppermute(value, "expert", pairs)


def swap_core(value):
    return lax.ppermute(value, "tensor", [(0, 1), (1, 0)])


def matmul(left, right):
    return jnp.dot(left, right, preferred_element_type=jnp.float32)


def gather_rows(block):
    half = block.shape[0] // 2
    from_z = [block] + [across(block, TURN_UP[k]) for k in range(1, 4)]
    groups = []
    for k in range(4):
        first, second = from_z[k][:half], from_z[k][half:]
        first_x = across(first, FLIP_X)
        second_y = across(second, FLIP_Y)
        first_pair = jnp.concatenate([first, first_x])
        second_pair = jnp.concatenate([second, second_y])
        groups.append((first_pair, across(first_pair, FLIP_Y), second_pair, across(second_pair, FLIP_X)))
    return groups


def gather_weights(table):
    half = table.shape[1] // 2
    stack = jnp.stack([table] + [across(table, TURN_UP[k]) for k in range(1, 4)])
    with_x = jnp.stack([stack, across(stack, FLIP_X)])
    with_y = jnp.stack([with_x, across(with_x, FLIP_Y)])
    mine = lax.dynamic_index_in_dim(with_y, lax.axis_index("expert"), 3, keepdims=False)
    columns = []
    for k in range(4):
        first, second = mine[:, :, k, :half], mine[:, :, k, half:]
        order = [first[0, 0], first[0, 1], first[1, 0], first[1, 1]]
        order += [second[0, 0], second[1, 0], second[0, 1], second[1, 1]]
        columns.append(jnp.concatenate(order)[:, None])
    return columns


def add_low(left, right):
    return (left.astype(jnp.float32) + right.astype(jnp.float32)).astype(jnp.bfloat16)


def return_group(rows, k):
    part = rows.shape[0] // 4
    half = part // 2
    first = add_low(rows[:part], across(rows[part : 2 * part], FLIP_Y))
    second = add_low(rows[2 * part : 3 * part], across(rows[3 * part :], FLIP_X))
    first_sum = add_low(first[:half], across(first[half:], FLIP_X))
    second_sum = add_low(second[:half], across(second[half:], FLIP_Y))
    total = jnp.concatenate([first_sum, second_sum])
    return across(total, TURN_DOWN[k]) if k else total


def expert_kernel(
    rows_ref,
    grad_ref,
    weight_ref,
    gate_ref,
    up_ref,
    down_ref,
    gate_t_ref,
    up_t_ref,
    down_t_ref,
    hidden_ref,
    act_grad_ref,
    out_ref,
    input_ref,
):
    rows = rows_ref[...]
    weight = weight_ref[...]
    width = hidden_ref.shape[1]
    gate = matmul(rows, gate_ref[...])
    up = matmul(rows, up_ref[...])
    grad_hidden = matmul(grad_ref[...], down_t_ref[...]) * weight
    logistic = 1.0 / (1.0 + jnp.exp(-gate))
    activated = gate * logistic
    hidden_ref[...] = (activated * up * weight).astype(jnp.bfloat16)
    grad_gate = (grad_hidden * up * logistic * (1.0 + gate * (1.0 - logistic))).astype(jnp.bfloat16)
    grad_up = (grad_hidden * activated).astype(jnp.bfloat16)
    act_grad_ref[:, :width] = grad_gate
    act_grad_ref[:, width:] = grad_up
    input_ref[...] = (matmul(grad_gate, gate_t_ref[...]) + matmul(grad_up, up_t_ref[...])).astype(
        jnp.bfloat16
    )
    out_ref[...] = matmul(hidden_ref[...], down_ref[...]).astype(jnp.bfloat16)


def expert_rows_call(rows, grads, weight, mats):
    count, width = rows.shape
    hidden = mats[0].shape[1]
    tile = 256
    row_spec = lambda columns: pl.BlockSpec((tile, columns), lambda i: (i, 0))
    whole = lambda mat: pl.BlockSpec(mat.shape, lambda i: (0, 0))
    return pl.pallas_call(
        expert_kernel,
        grid=(count // tile,),
        in_specs=[row_spec(width), row_spec(width), row_spec(1)] + [whole(mat) for mat in mats],
        out_specs=[row_spec(hidden), row_spec(2 * hidden), row_spec(width), row_spec(width)],
        out_shape=[
            jax.ShapeDtypeStruct((count, hidden), jnp.bfloat16),
            jax.ShapeDtypeStruct((count, 2 * hidden), jnp.bfloat16),
            jax.ShapeDtypeStruct((count, width), jnp.bfloat16),
            jax.ShapeDtypeStruct((count, width), jnp.bfloat16),
        ],
        compiler_params=pltpu.CompilerParams(vmem_limit_bytes=60 << 20),
        cost_estimate=pl.CostEstimate(
            flops=12 * count * width * hidden,
            bytes_accessed=2 * (4 * count * width + 3 * count * hidden + 6 * width * hidden),
            transcendentals=count * hidden,
        ),
        name="expert_rows",
    )(rows, grads, weight, *mats)


def contract(left, right):
    return lax.dot_general(left, right, (((1,), (1,)), ((), ())), preferred_element_type=jnp.float32)


def small_solve_kernel(matrix_ref, scale_ref, ortho_ref):
    count = matrix_ref.shape[0]
    for index in range(count):
        ortho_ref[index] = (matrix_ref[index].astype(jnp.float32) * scale_ref[index]).astype(jnp.bfloat16)
        for _ in range(NS_ITERS):
            iterate = ortho_ref[index]
            gram = contract(iterate, iterate).astype(jnp.bfloat16)
            square = matmul(gram, gram)
            poly = (coeff_two * gram.astype(jnp.float32) + coeff_three * square).astype(jnp.bfloat16)
            ortho_ref[index] = (
                coeff_one * iterate.astype(jnp.float32) + matmul(poly, iterate)
            ).astype(jnp.bfloat16)


def small_solve(matrices):
    scale = inverse_norm(matrices)
    count, rows, columns = matrices.shape
    return pl.pallas_call(
        small_solve_kernel,
        out_shape=jax.ShapeDtypeStruct(matrices.shape, jnp.bfloat16),
        in_specs=[
            pl.BlockSpec(memory_space=pltpu.VMEM),
            pl.BlockSpec(memory_space=pltpu.SMEM),
        ],
        out_specs=pl.BlockSpec(memory_space=pltpu.VMEM),
        compiler_params=pltpu.CompilerParams(vmem_limit_bytes=60 << 20),
        cost_estimate=pl.CostEstimate(
            flops=count * NS_ITERS * 2 * rows * rows * (2 * columns + rows),
            bytes_accessed=4 * count * rows * columns,
            transcendentals=0,
        ),
        name="small_solve",
    )(matrices, scale)


def inverse_norm(matrices):
    wide = matrices.astype(jnp.float32)
    return 1.0 / (jnp.sqrt(jnp.sum(wide * wide, axis=(1, 2))) + 1e-07)


def start_of(matrix):
    wide = matrix.astype(jnp.float32)
    return (wide * (1.0 / (jnp.sqrt(jnp.sum(wide * wide)) + 1e-07))).astype(jnp.bfloat16)


def full_step(iterate):
    gram = contract(iterate, iterate).astype(jnp.bfloat16)
    square = matmul(gram, gram)
    poly = (coeff_two * gram.astype(jnp.float32) + coeff_three * square).astype(jnp.bfloat16)
    return (coeff_one * iterate.astype(jnp.float32) + matmul(poly, iterate)).astype(jnp.bfloat16)


def column_step(iterate, start, count):
    picked = lax.dynamic_slice_in_dim(iterate, start, count, 1)
    back = lambda value: lax.dot_general(
        iterate, value, (((0,), (0,)), ((), ())), preferred_element_type=jnp.float32
    ).astype(jnp.bfloat16)
    once = matmul(iterate, back(picked))
    twice = matmul(iterate, back(once.astype(jnp.bfloat16)))
    return (coeff_one * picked.astype(jnp.float32) + coeff_two * once + coeff_three * twice).astype(jnp.bfloat16)


def sum_shards(payload, first_y):
    chip = lax.axis_index("expert")
    z, y, x = chip // 4, chip // 2 % 2, chip % 2
    rows = payload.shape[0] // 16
    cut = payload.reshape(4, 2, 2, rows, payload.shape[1])

    def halve(value, axis, at, pairs):
        keep = lax.dynamic_index_in_dim(value, at, axis, keepdims=False)
        send = lax.dynamic_index_in_dim(value, 1 - at, axis, keepdims=False)
        return add_low(keep, across(send, pairs))

    if first_y:
        cut = halve(halve(cut, 1, y, FLIP_Y), 1, x, FLIP_X)
    else:
        cut = halve(halve(cut, 2, x, FLIP_X), 1, y, FLIP_Y)
    total = lax.dynamic_index_in_dim(cut, z, 0, keepdims=False).astype(jnp.float32)
    for k in range(1, 4):
        send = lax.dynamic_index_in_dim(cut, (z + 4 - k) % 4, 0, keepdims=False)
        total = total + across(send, TURN_DOWN[k]).astype(jnp.float32)
    return total.astype(jnp.bfloat16)


def join_shards(shard, first_y):
    chip = lax.axis_index("expert")
    z, y, x = chip // 4, chip // 2 % 2, chip % 2
    moved = [shard] + [across(shard, TURN_UP[k]) for k in range(1, 4)]
    turn = [moved[0], moved[3], moved[2], moved[1]]
    stack = lax.dynamic_slice_in_dim(jnp.stack(turn + turn[:3]), (4 - z) % 4, 4, 0)

    def double(value, axis, at, pairs):
        other = across(value, pairs)
        return jnp.where(at == 0, jnp.stack([value, other], axis), jnp.stack([other, value], axis))

    if first_y:
        whole = double(double(stack, 1, x, FLIP_X), 1, y, FLIP_Y)
    else:
        whole = double(double(stack, 1, y, FLIP_Y), 2, x, FLIP_X)
    return whole.reshape(-1, shard.shape[1])


def sum_everywhere(value):
    value = value + swap_core(value)
    for pairs in (FLIP_X, FLIP_Y, FLIP_Z1, FLIP_Z2):
        value = value + across(value, pairs)
    return value


def own_half(value, axis=0):
    size = value.shape[axis] // 2
    return lax.dynamic_slice_in_dim(value, lax.axis_index("tensor") * size, size, axis)


def other_half(value, axis=0):
    size = value.shape[axis] // 2
    return lax.dynamic_slice_in_dim(value, (1 - lax.axis_index("tensor")) * size, size, axis)


def both_halves(value):
    other = swap_core(value)
    first = lax.axis_index("tensor") == 0
    return jnp.concatenate([jnp.where(first, value, other), jnp.where(first, other, value)])


def per_core(
    block_in,
    segments,
    routes,
    route_weights,
    gain_attn,
    gain_ffn,
    w_query,
    w_key,
    w_value,
    w_out_proj,
    w_gate,
    w_up,
    w_down,
    mom_query,
    mom_key,
    mom_value,
    mom_out_proj,
    mom_gate,
    mom_up,
    mom_down,
    mom_gain_attn,
    mom_gain_ffn,
    cotangent,
):
    tok_rows, width = block_in.shape
    experts = lax.axis_size("expert")
    tensor_pos = lax.axis_index("tensor")
    expert_pos = lax.axis_index("expert")
    first_core = tensor_pos == 0

    own_top = own_half(cotangent)
    top_groups = gather_rows(own_top)
    own_routes = own_half(routes)
    own_scales = own_half(route_weights)
    named = own_routes[None] == jnp.arange(experts, dtype=jnp.int32)[:, None, None]
    table = jnp.sum(jnp.where(named, own_scales[None], 0.0), axis=2)
    columns = gather_weights(table)
    expert_mats = jnp.concatenate([w_gate[0], w_up[0]], axis=1)
    other_mats = swap_core(expert_mats)
    half = w_gate.shape[2]
    gate_mat = jnp.concatenate([w_gate[0], other_mats[:, :half]], axis=1)
    up_mat = jnp.concatenate([w_up[0], other_mats[:, half:]], axis=1)
    down_mat = jnp.concatenate([w_down[0], swap_core(w_down[0])], axis=0)
    mats = (gate_mat, up_mat, down_mat, gate_mat.T, up_mat.T, down_mat.T)

    residual_in = block_in.astype(jnp.float32)
    inv_first = lax.rsqrt(jnp.mean(residual_in * residual_in, axis=1, keepdims=True) + norm_eps)
    normed_attn = (residual_in * inv_first * gain_attn).astype(jnp.bfloat16)
    queries = (matmul(normed_attn, w_query) * HD ** (-0.5)).astype(jnp.bfloat16)
    key_rows = matmul(normed_attn, w_key).astype(jnp.bfloat16)
    value_rows = matmul(normed_attn, w_value).astype(jnp.bfloat16)
    log_total, attn_mixed = attend_forward((queries, key_rows, value_rows, segments))
    attn_part = matmul(attn_mixed, w_out_proj)
    own_in = own_half(residual_in)
    hidden_state = (
        own_in
        + own_half(attn_part)
        + swap_core(other_half(attn_part).astype(jnp.bfloat16)).astype(jnp.float32)
    )
    inv_second = lax.rsqrt(jnp.mean(hidden_state * hidden_state, axis=1, keepdims=True) + norm_eps)
    normed_ffn = (hidden_state * inv_second * gain_ffn).astype(jnp.bfloat16)

    row_groups = gather_rows(normed_ffn)
    hidden_parts, grad_parts, out_parts, back_parts, rows_all, tops_all = [], [], [], [], [], []
    for k in range(4):
        rows = jnp.concatenate(row_groups[k])
        tops = jnp.concatenate(top_groups[k])
        hidden, act_grads, out_rows, input_rows = expert_rows_call(rows, tops, columns[k], mats)
        back_parts.append(return_group(input_rows, k))
        out_parts.append(out_rows)
        hidden_parts.append(hidden)
        grad_parts.append(act_grads)
        rows_all.append(rows)
        tops_all.append(tops)
    grad_normed_ffn = sum(part.astype(jnp.float32) for part in back_parts)
    moe_sum = sum(return_group(out_parts[k], k).astype(jnp.float32) for k in range(4))
    block_out = both_halves((hidden_state + moe_sum).astype(jnp.bfloat16))

    over_rows = lambda left, right: lax.dot_general(
        left, right, (((0,), (0,)), ((), ())), preferred_element_type=jnp.float32
    )
    grad_pair = sum(over_rows(rows_all[k], grad_parts[k]) for k in range(4))
    grad_down_all = sum(over_rows(hidden_parts[k], tops_all[k]) for k in range(4))
    ff = 2 * half
    send_pair = jnp.concatenate([grad_pair[:, half:ff], grad_pair[:, ff + half :]], axis=1).astype(jnp.bfloat16)
    got_pair = swap_core(send_pair).astype(jnp.float32)
    grad_gate = grad_pair[:, :half] + got_pair[:, :half]
    grad_up = grad_pair[:, ff : ff + half] + got_pair[:, half:]
    grad_down = grad_down_all[:half] + swap_core(grad_down_all[half:].astype(jnp.bfloat16)).astype(jnp.float32)
    new_mom_gate = momentum_decay * mom_gate + grad_gate[None]
    new_mom_up = momentum_decay * mom_up + grad_up[None]
    new_mom_down = momentum_decay * mom_down + grad_down[None]
    gate_rows = new_mom_gate[0].astype(jnp.bfloat16).T
    up_rows = new_mom_up[0].astype(jnp.bfloat16).T
    down_rows = new_mom_down[0].astype(jnp.bfloat16)
    keep_rows = jnp.where(first_core, gate_rows, up_rows)
    send_rows = jnp.where(first_core, up_rows, gate_rows)
    problems = jnp.stack(
        [
            jnp.concatenate([keep_rows, swap_core(send_rows)]),
            jnp.concatenate([down_rows, swap_core(down_rows)]),
        ]
    )
    solved = small_solve(problems)
    got_ortho = swap_core(solved[0, half:])
    ortho_gate = jnp.where(first_core, solved[0, :half], got_ortho).T
    ortho_up = jnp.where(first_core, got_ortho, solved[0, :half]).T
    ortho_down = solved[1, :half]

    def apply_update(weight, ortho_piece, larger):
        factor = learn_rate * 0.2 * math.sqrt(larger)
        return weight.astype(jnp.float32) - factor * ortho_piece.astype(jnp.float32)

    new_gate = apply_update(w_gate, ortho_gate[None], max(width, ff))
    new_up = apply_update(w_up, ortho_up[None], max(width, ff))
    new_down = apply_update(w_down, ortho_down[None], max(width, ff))

    gain_ffn_part = jnp.sum(grad_normed_ffn * hidden_state * inv_second, axis=0)
    scaled = grad_normed_ffn * gain_ffn
    grad_state = own_top.astype(jnp.float32) + inv_second * (
        scaled
        - hidden_state
        * inv_second
        * inv_second
        * jnp.mean(scaled * hidden_state, axis=1, keepdims=True)
    )
    grad_state_low = both_halves(grad_state.astype(jnp.bfloat16))
    grad_mixed = contract(grad_state_low, w_out_proj).astype(jnp.bfloat16)
    grad_queries, grad_keys, grad_values = attend_backward(
        (queries, key_rows, value_rows, segments, log_total, attn_mixed, grad_mixed)
    )
    grad_out_local = over_rows(attn_mixed, grad_state_low)
    grad_query_local = over_rows(normed_attn, grad_queries)
    grad_key_local = over_rows(normed_attn, grad_keys)
    grad_value_local = over_rows(grad_values, normed_attn)
    first_payload = jnp.concatenate([grad_query_local, grad_key_local], axis=1).astype(jnp.bfloat16)
    second_payload = jnp.concatenate([grad_out_local, grad_value_local], axis=0).astype(jnp.bfloat16)
    first_sum = join_shards(sum_shards(first_payload, True), True)
    second_sum = join_shards(sum_shards(second_payload, False), False)

    attn_input_part = (
        contract(grad_queries, w_query) + contract(grad_keys, w_key) + contract(grad_values, w_value)
    )
    grad_normed_attn = own_half(attn_input_part) + swap_core(
        other_half(attn_input_part).astype(jnp.bfloat16)
    ).astype(jnp.float32)
    own_inv = own_half(inv_first)
    gain_attn_part = jnp.sum(grad_normed_attn * own_in * own_inv, axis=0)
    scaled_first = grad_normed_attn * gain_attn
    grad_input = both_halves(
        grad_state
        + own_inv
        * (
            scaled_first
            - own_in
            * own_inv
            * own_inv
            * jnp.mean(scaled_first * own_in, axis=1, keepdims=True)
        )
    )
    gain_sums = sum_everywhere(jnp.stack([gain_attn_part, gain_ffn_part]))
    grad_gain_attn, grad_gain_ffn = gain_sums[0], gain_sums[1]

    query_cols, key_cols = w_query.shape[1], w_key.shape[1]
    out_rows_count = w_out_proj.shape[0]
    grad_query = first_sum[:, :query_cols].astype(jnp.float32)
    grad_key = first_sum[:, query_cols:].astype(jnp.float32)
    grad_out_proj = second_sum[:out_rows_count].astype(jnp.float32)
    grad_value = second_sum[out_rows_count:].T.astype(jnp.float32)
    new_mom_query = momentum_decay * mom_query + grad_query
    new_mom_key = momentum_decay * mom_key + grad_key
    new_mom_value = momentum_decay * mom_value + grad_value
    new_mom_out_proj = momentum_decay * mom_out_proj + grad_out_proj
    new_mom_gain_attn = momentum_decay * mom_gain_attn + grad_gain_attn
    new_mom_gain_ffn = momentum_decay * mom_gain_ffn + grad_gain_ffn

    query_rows = new_mom_query.astype(jnp.bfloat16).T
    out_proj_rows = new_mom_out_proj.astype(jnp.bfloat16)
    large_keep = jnp.where(first_core, query_rows, out_proj_rows)
    large_send = jnp.where(first_core, out_proj_rows, query_rows)
    key_t = new_mom_key.astype(jnp.bfloat16).T
    value_t = new_mom_value.astype(jnp.bfloat16).T
    small_keep = jnp.where(first_core, key_t, value_t)
    small_send = jnp.where(first_core, value_t, key_t)
    large = start_of(jnp.concatenate([large_keep, swap_core(large_send)]))
    small = start_of(jnp.concatenate([small_keep, swap_core(small_send)]))
    piece = width // experts
    large_cols = column_step(full_step(full_step(large)), expert_pos * piece, piece)
    small_cols = column_step(full_step(full_step(small)), expert_pos * piece, piece)
    got_large = swap_core(large_cols[out_rows_count:])
    got_small = swap_core(small_cols[key_cols:])
    query_piece = jnp.where(first_core, large_cols[:out_rows_count], got_large).T
    out_piece = jnp.where(first_core, got_large, large_cols[:out_rows_count])
    key_piece = jnp.where(first_core, small_cols[:key_cols], got_small).T
    value_piece = jnp.where(first_core, got_small, small_cols[:key_cols]).T

    def expert_rows(matrix, along_dim):
        return lax.dynamic_slice_in_dim(matrix, expert_pos * piece, piece, along_dim)

    new_query = apply_update(expert_rows(w_query, 0), query_piece, width)
    new_key = apply_update(expert_rows(w_key, 0), key_piece, width)
    new_value = apply_update(expert_rows(w_value, 0), value_piece, width)
    new_out_proj = apply_update(expert_rows(w_out_proj, 1), out_piece, width)
    new_gain_attn = gain_attn - gain_rate * new_mom_gain_attn
    new_gain_ffn = gain_ffn - gain_rate * new_mom_gain_ffn
    return (
        block_out,
        grad_input,
        grad_query,
        grad_key,
        grad_value,
        grad_out_proj,
        grad_gate[None],
        grad_up[None],
        grad_down[None],
        grad_gain_attn,
        grad_gain_ffn,
        new_query,
        new_key,
        new_value,
        new_out_proj,
        new_gate,
        new_up,
        new_down,
        new_gain_attn,
        new_gain_ffn,
        new_mom_query,
        new_mom_key,
        new_mom_value,
        new_mom_out_proj,
        new_mom_gate,
        new_mom_up,
        new_mom_down,
        new_mom_gain_attn,
        new_mom_gain_ffn,
    )


def solution(mesh):
    placed = (
        P("expert", None),
        P("expert"),
        P("expert", None),
        P("expert", None),
        P(),
        P(),
        P(None, "tensor"),
        P(None, "tensor"),
        P(None, "tensor"),
        P("tensor", None),
        P("expert", None, "tensor"),
        P("expert", None, "tensor"),
        P("expert", "tensor", None),
        P(None, "tensor"),
        P(None, "tensor"),
        P(None, "tensor"),
        P("tensor", None),
        P("expert", None, "tensor"),
        P("expert", None, "tensor"),
        P("expert", "tensor", None),
        P(),
        P(),
        P("expert", None),
    )
    blocked = mesh.shape["expert"] == 16 and mesh.shape["tensor"] == 2
    return jax.shard_map(
        per_core if blocked else per_device,
        mesh=mesh,
        in_specs=placed,
        out_specs=(
            P("expert", None),
            P("expert", None),
            P(None, "tensor"),
            P(None, "tensor"),
            P(None, "tensor"),
            P("tensor", None),
            P("expert", None, "tensor"),
            P("expert", None, "tensor"),
            P("expert", "tensor", None),
            P(),
            P(),
            P("expert", "tensor"),
            P("expert", "tensor"),
            P("expert", "tensor"),
            P("tensor", "expert"),
            P("expert", None, "tensor"),
            P("expert", None, "tensor"),
            P("expert", "tensor", None),
            P(),
            P(),
            P(None, "tensor"),
            P(None, "tensor"),
            P(None, "tensor"),
            P("tensor", None),
            P("expert", None, "tensor"),
            P("expert", None, "tensor"),
            P("expert", "tensor", None),
            P(),
            P(),
        ),
        check_vma=False,
    )
```

```python
import functools
import math

import jax
import jax.numpy as jnp
from jax import lax
from jax.experimental import pallas as pl
from jax.experimental.layout import Layout, with_layout_constraint
from jax.experimental.pallas import tpu as pltpu
from jax.sharding import PartitionSpec as P

HD = 64
TOPK = 8
SEQ = 512
NS_ITERS = 3


momentum_decay = 0.95
learn_rate = 0.2
gain_rate = 0.002
norm_eps = 1e-05
coeff_one = 3.4445
coeff_two = -4.775
coeff_three = 2.0315


def shortened(value):

    def short(part):
        return part.astype(jnp.bfloat16) if part.dtype == jnp.float32 else part

    return jax.tree.map(short, value)


def spread(value, axis, root):
    mine = lax.axis_index(axis) == root
    return lax.psum(jnp.where(mine, value, jnp.zeros_like(value)), axis)


def silu_grad(values):
    logistic = jax.nn.sigmoid(values)
    return logistic * (1.0 + values * (1.0 - logistic))


def causal_mask(seg_ids):
    length = seg_ids.shape[0]
    row_pos = lax.broadcasted_iota(jnp.int32, (length, length), 0)
    col_pos = lax.broadcasted_iota(jnp.int32, (length, length), 1)
    return (col_pos <= row_pos) & (seg_ids[:, None] == seg_ids[None, :])


def group_scores(queries, key_rows, mask):
    length = queries.shape[0]
    groups = key_rows.shape[1] // HD
    query_heads = queries.reshape(length, groups, -1, HD)
    key_heads = key_rows.reshape(length, groups, HD)
    scores = jnp.einsum(
        "skgd,tkd->kgst", query_heads, key_heads, preferred_element_type=jnp.float32
    )
    return jnp.where(mask[None, None], scores, -jnp.inf)


def attend_forward(bundle):
    queries, key_rows, value_rows, seg_ids = bundle
    length = queries.shape[0]
    groups = key_rows.shape[1] // HD
    scores = group_scores(queries, key_rows, causal_mask(seg_ids))
    highest = jnp.max(scores, axis=3, keepdims=True)
    log_total = highest + jnp.log(jnp.sum(jnp.exp(scores - highest), axis=3, keepdims=True))
    attn_probs = jnp.exp(scores - log_total).astype(jnp.bfloat16)
    attn_mixed = jnp.einsum(
        "kgst,tkd->skgd",
        attn_probs,
        value_rows.reshape(length, groups, HD),
        preferred_element_type=jnp.float32,
    )
    return (log_total, attn_mixed.reshape(length, -1).astype(jnp.bfloat16))


def attend_backward(bundle):
    queries, key_rows, value_rows, seg_ids, log_total, attn_mixed, grad_mixed = bundle
    length = queries.shape[0]
    groups = key_rows.shape[1] // HD
    scores = group_scores(queries, key_rows, causal_mask(seg_ids))
    probs_full = jnp.exp(scores - log_total)
    attn_probs = probs_full.astype(jnp.bfloat16)
    grad_heads = grad_mixed.reshape(length, groups, -1, HD)
    grad_probs = jnp.einsum(
        "skgd,tkd->kgst",
        grad_heads,
        value_rows.reshape(length, groups, HD),
        preferred_element_type=jnp.float32,
    )
    offset = jnp.einsum(
        "skgd,skgd->kgs",
        grad_heads,
        attn_mixed.reshape(length, groups, -1, HD),
        preferred_element_type=jnp.float32,
    )
    grad_scores = (probs_full * (grad_probs - offset[..., None])).astype(jnp.bfloat16)
    grad_queries = jnp.einsum(
        "kgst,tkd->skgd",
        grad_scores,
        key_rows.reshape(length, groups, HD),
        preferred_element_type=jnp.float32,
    )
    grad_queries = (grad_queries * HD ** (-0.5)).reshape(length, -1).astype(jnp.bfloat16)
    grad_keys = jnp.einsum(
        "kgst,skgd->tkd",
        grad_scores,
        queries.reshape(length, groups, -1, HD),
        preferred_element_type=jnp.float32,
    )
    grad_values = jnp.einsum(
        "kgst,skgd->tkd", attn_probs, grad_heads, preferred_element_type=jnp.float32
    )
    return (
        grad_queries,
        grad_keys.reshape(length, -1).astype(jnp.bfloat16),
        grad_values.reshape(length, -1).astype(jnp.bfloat16),
    )


def newton_schulz(matrix):
    flipped = matrix.shape[0] > matrix.shape[1]
    oriented = matrix.T if flipped else matrix
    frob_norm = jnp.sqrt(jnp.sum(oriented * oriented)) + 1e-07
    iterate = (oriented / frob_norm).astype(jnp.bfloat16)
    for sweep_index in range(NS_ITERS):
        gram_mat = jnp.dot(iterate, iterate.T, preferred_element_type=jnp.float32).astype(
            jnp.bfloat16
        )
        square = jnp.dot(gram_mat, gram_mat, preferred_element_type=jnp.float32)
        poly_mix = (coeff_two * gram_mat.astype(jnp.float32) + coeff_three * square).astype(
            jnp.bfloat16
        )
        iterate = (
            coeff_one * iterate.astype(jnp.float32)
            + jnp.dot(poly_mix, iterate, preferred_element_type=jnp.float32)
        ).astype(jnp.bfloat16)
    return iterate.T if flipped else iterate


def zero_ortho(matrix):
    return jnp.zeros(matrix.shape, jnp.bfloat16)


def solve_set(which_set):

    def solve_branch(matrices):
        return tuple(
            (
                (
                    newton_schulz(matrices[index])
                    if index in which_set
                    else zero_ortho(matrices[index])
                )
                for index in range(len(matrices))
            )
        )

    return solve_branch


def per_device(
    block_in,
    segments,
    routes,
    route_weights,
    gain_attn,
    gain_ffn,
    w_query,
    w_key,
    w_value,
    w_out_proj,
    w_gate,
    w_up,
    w_down,
    mom_query,
    mom_key,
    mom_value,
    mom_out_proj,
    mom_gate,
    mom_up,
    mom_down,
    mom_gain_attn,
    mom_gain_ffn,
    cotangent,
):
    tok_rows, width = block_in.shape
    seq_count = tok_rows // SEQ
    tensor_count = lax.axis_size("tensor")
    expert_count = lax.axis_size("expert")
    tensor_pos = lax.axis_index("tensor")
    expert_pos = lax.axis_index("expert")
    residual_in = block_in.astype(jnp.float32)
    inv_first = lax.rsqrt(jnp.mean(residual_in * residual_in, axis=1, keepdims=True) + norm_eps)
    normed_attn = (residual_in * inv_first * gain_attn).astype(jnp.bfloat16)
    queries = (
        jnp.dot(normed_attn, w_query, preferred_element_type=jnp.float32) * HD ** (-0.5)
    ).astype(jnp.bfloat16)
    key_rows = jnp.dot(normed_attn, w_key, preferred_element_type=jnp.float32).astype(jnp.bfloat16)
    value_rows = jnp.dot(normed_attn, w_value, preferred_element_type=jnp.float32).astype(
        jnp.bfloat16
    )
    seq_items = (
        queries.reshape(seq_count, SEQ, -1),
        key_rows.reshape(seq_count, SEQ, -1),
        value_rows.reshape(seq_count, SEQ, -1),
        segments.reshape(seq_count, SEQ),
    )
    log_total, attn_mixed = lax.map(attend_forward, seq_items)
    mixed_flat = attn_mixed.reshape(tok_rows, -1)
    attn_part = jnp.dot(mixed_flat, w_out_proj, preferred_element_type=jnp.float32)
    hidden_state = residual_in + lax.psum(attn_part.astype(jnp.bfloat16), "tensor").astype(
        jnp.float32
    )
    inv_second = lax.rsqrt(jnp.mean(hidden_state * hidden_state, axis=1, keepdims=True) + norm_eps)
    normed_ffn = (hidden_state * inv_second * gain_ffn).astype(jnp.bfloat16)
    capacity = min(tok_rows, 5 * tok_rows * TOPK // (4 * expert_count) // 8 * 8)
    quarter_cap = capacity // tensor_count
    flat_routes = routes.reshape(-1)
    flat_weights = route_weights.reshape(-1)
    one_hot = (flat_routes[:, None] == jnp.arange(expert_count, dtype=jnp.int32)[None, :]).astype(
        jnp.int32
    )
    route_rank = jnp.sum((jnp.cumsum(one_hot, axis=0) - one_hot) * one_hot, axis=1)
    slot_ids = flat_routes * capacity + route_rank
    local_rank = route_rank - tensor_pos * quarter_cap
    inside = (local_rank >= 0) & (local_rank < quarter_cap)
    quarter_ids = flat_routes * quarter_cap + jnp.clip(local_rank, 0, quarter_cap - 1)

    def place_rows(row_values):
        slot_table = jnp.zeros((expert_count * capacity, width), jnp.bfloat16)
        return slot_table.at[slot_ids].set(row_values).reshape(expert_count, capacity, width)

    grad_top = cotangent.astype(jnp.float32)
    grad_routed = (jnp.repeat(grad_top, TOPK, axis=0) * flat_weights[:, None]).astype(jnp.bfloat16)
    routed_rows = place_rows(jnp.repeat(normed_ffn, TOPK, axis=0))
    received = lax.all_to_all(routed_rows, "expert", split_axis=0, concat_axis=0, tiled=True)
    flat_rows = received.reshape(-1, width)
    gate_act = jnp.dot(flat_rows, w_gate[0], preferred_element_type=jnp.float32)
    up_act = jnp.dot(flat_rows, w_up[0], preferred_element_type=jnp.float32)
    hidden = (jax.nn.silu(gate_act) * up_act).astype(jnp.bfloat16)
    expert_part = jnp.dot(hidden, w_down[0], preferred_element_type=jnp.float32).astype(
        jnp.bfloat16
    )
    expert_out = expert_part.reshape(received.shape)
    summed = lax.psum_scatter(
        expert_out.astype(jnp.float32).astype(jnp.bfloat16),
        "tensor",
        scatter_dimension=1,
        tiled=True,
    ).astype(jnp.float32)
    returned = lax.all_to_all(
        summed.astype(jnp.bfloat16), "expert", split_axis=0, concat_axis=0, tiled=True
    ).astype(summed.dtype)
    picked = (
        returned.reshape(-1, width)[quarter_ids] * jnp.where(inside, flat_weights, 0.0)[:, None]
    )
    moe_part = jnp.sum(picked.reshape(tok_rows, TOPK, width), axis=1)
    block_out = (
        hidden_state + lax.psum(moe_part.astype(jnp.bfloat16), "tensor").astype(jnp.float32)
    ).astype(jnp.bfloat16)
    grad_received = lax.all_to_all(
        place_rows(grad_routed), "expert", split_axis=0, concat_axis=0, tiled=True
    )
    flat_rows = received.reshape(-1, width)
    flat_grad = grad_received.reshape(-1, width)
    gate_act = jnp.dot(flat_rows, w_gate[0], preferred_element_type=jnp.float32)
    up_act = jnp.dot(flat_rows, w_up[0], preferred_element_type=jnp.float32)
    activated = jax.nn.silu(gate_act)
    hidden = (activated * up_act).astype(jnp.bfloat16)
    grad_hidden = jnp.dot(flat_grad, w_down[0].T, preferred_element_type=jnp.float32)
    grad_gate_act = (grad_hidden * up_act * silu_grad(gate_act)).astype(jnp.bfloat16)
    grad_up_act = (grad_hidden * activated).astype(jnp.bfloat16)
    grad_down = jnp.dot(hidden.T, flat_grad, preferred_element_type=jnp.float32)[None]
    grad_gate = jnp.dot(flat_rows.T, grad_gate_act, preferred_element_type=jnp.float32)[None]
    grad_up = jnp.dot(flat_rows.T, grad_up_act, preferred_element_type=jnp.float32)[None]
    input_part = jnp.dot(grad_gate_act, w_gate[0].T, preferred_element_type=jnp.float32)
    input_part = input_part + jnp.dot(grad_up_act, w_up[0].T, preferred_element_type=jnp.float32)
    input_part = input_part.astype(jnp.bfloat16).reshape(expert_count, capacity, width)
    summed_grad = lax.psum_scatter(
        input_part.astype(jnp.float32).astype(jnp.bfloat16),
        "tensor",
        scatter_dimension=1,
        tiled=True,
    ).astype(jnp.float32)
    returned_grad = lax.all_to_all(
        summed_grad.astype(jnp.bfloat16), "expert", split_axis=0, concat_axis=0, tiled=True
    ).astype(summed_grad.dtype)
    picked_grad = (
        returned_grad.reshape(-1, width)[quarter_ids] * inside.astype(jnp.float32)[:, None]
    )
    ffn_part = jnp.sum(picked_grad.reshape(tok_rows, TOPK, width), axis=1)
    grad_normed_ffn = lax.psum(ffn_part.astype(jnp.bfloat16), "tensor").astype(jnp.float32)
    gain_ffn_part = jnp.sum(grad_normed_ffn * hidden_state * inv_second, axis=0)
    scaled = grad_normed_ffn * gain_ffn
    grad_state = grad_top + inv_second * (
        scaled
        - hidden_state
        * inv_second
        * inv_second
        * jnp.mean(scaled * hidden_state, axis=1, keepdims=True)
    )
    grad_state_low = grad_state.astype(jnp.bfloat16)
    grad_out_local = jnp.dot(mixed_flat.T, grad_state_low, preferred_element_type=jnp.float32)
    grad_mixed = jnp.dot(grad_state_low, w_out_proj.T, preferred_element_type=jnp.float32).astype(
        jnp.bfloat16
    )
    back_items = seq_items + (log_total, attn_mixed, grad_mixed.reshape(seq_count, SEQ, -1))
    grad_queries, grad_keys, grad_values = lax.map(attend_backward, back_items)
    grad_queries = grad_queries.reshape(tok_rows, -1)
    grad_keys = grad_keys.reshape(tok_rows, -1)
    grad_values = grad_values.reshape(tok_rows, -1)
    grad_query_local = jnp.dot(normed_attn.T, grad_queries, preferred_element_type=jnp.float32)
    grad_key_local = jnp.dot(normed_attn.T, grad_keys, preferred_element_type=jnp.float32)
    grad_value_local = jnp.dot(normed_attn.T, grad_values, preferred_element_type=jnp.float32)
    attn_input_part = jnp.dot(grad_queries, w_query.T, preferred_element_type=jnp.float32)
    attn_input_part = attn_input_part + jnp.dot(
        grad_keys, w_key.T, preferred_element_type=jnp.float32
    )
    attn_input_part = attn_input_part + jnp.dot(
        grad_values, w_value.T, preferred_element_type=jnp.float32
    )
    grad_normed_attn = lax.psum(attn_input_part.astype(jnp.bfloat16), "tensor").astype(jnp.float32)
    gain_attn_part = jnp.sum(grad_normed_attn * residual_in * inv_first, axis=0)
    scaled_first = grad_normed_attn * gain_attn
    grad_input = grad_state + inv_first * (
        scaled_first
        - residual_in
        * inv_first
        * inv_first
        * jnp.mean(scaled_first * residual_in, axis=1, keepdims=True)
    )
    grad_query, grad_key, grad_value, grad_out_proj, grad_gain_attn, grad_gain_ffn = (
        lax.psum(grad_query_local.astype(jnp.bfloat16), "expert").astype(jnp.float32),
        lax.psum(grad_key_local.astype(jnp.bfloat16), "expert").astype(jnp.float32),
        lax.psum(grad_value_local.astype(jnp.bfloat16), "expert").astype(jnp.float32),
        lax.psum(grad_out_local.astype(jnp.bfloat16), "expert").astype(jnp.float32),
        lax.psum(gain_attn_part.astype(jnp.bfloat16), "expert").astype(jnp.float32),
        lax.psum(gain_ffn_part.astype(jnp.bfloat16), "expert").astype(jnp.float32),
    )
    new_mom_query = momentum_decay * mom_query + grad_query
    new_mom_key = momentum_decay * mom_key + grad_key
    new_mom_value = momentum_decay * mom_value + grad_value
    new_mom_out_proj = momentum_decay * mom_out_proj + grad_out_proj
    new_mom_gate = momentum_decay * mom_gate + grad_gate
    new_mom_up = momentum_decay * mom_up + grad_up
    new_mom_down = momentum_decay * mom_down + grad_down
    new_mom_gain_attn = momentum_decay * mom_gain_attn + grad_gain_attn
    new_mom_gain_ffn = momentum_decay * mom_gain_ffn + grad_gain_ffn
    gathered = (
        lax.all_gather(new_mom_query.astype(jnp.bfloat16), "tensor", axis=1, tiled=True).astype(
            new_mom_query.dtype
        ),
        lax.all_gather(new_mom_key.astype(jnp.bfloat16), "tensor", axis=1, tiled=True).astype(
            new_mom_key.dtype
        ),
        lax.all_gather(new_mom_value.astype(jnp.bfloat16), "tensor", axis=1, tiled=True).astype(
            new_mom_value.dtype
        ),
        lax.all_gather(new_mom_out_proj.astype(jnp.bfloat16), "tensor", axis=0, tiled=True).astype(
            new_mom_out_proj.dtype
        ),
        lax.all_gather(new_mom_gate.astype(jnp.bfloat16), "tensor", axis=2, tiled=True).astype(
            new_mom_gate.dtype
        ),
        lax.all_gather(new_mom_up.astype(jnp.bfloat16), "tensor", axis=2, tiled=True).astype(
            new_mom_up.dtype
        ),
        lax.all_gather(new_mom_down.astype(jnp.bfloat16), "tensor", axis=1, tiled=True).astype(
            new_mom_down.dtype
        ),
    )

    def expert_rows(matrix, along_dim):
        row_width = matrix.shape[along_dim] // expert_count
        return lax.dynamic_slice_in_dim(matrix, expert_pos * row_width, row_width, along_dim)

    def apply_update(weight, ortho_piece, whole_shape):
        factor = learn_rate * 0.2 * math.sqrt(max(whole_shape[-2], whole_shape[-1]))
        return weight.astype(jnp.float32) - factor * ortho_piece.astype(jnp.float32)

    expert_branches = [
        solve_set(tuple((index for index in range(3) if index % tensor_count == position)))
        for position in range(tensor_count)
    ]
    ortho_gate, ortho_up, ortho_down = lax.switch(
        tensor_pos, expert_branches, (gathered[4][0], gathered[5][0], gathered[6][0])
    )
    piece_gate, piece_up, piece_down = (
        lax.psum_scatter(
            ortho_gate[None].astype(jnp.bfloat16), "tensor", scatter_dimension=2, tiled=True
        ).astype(jnp.float32),
        lax.psum_scatter(
            ortho_up[None].astype(jnp.bfloat16), "tensor", scatter_dimension=2, tiled=True
        ).astype(jnp.float32),
        lax.psum_scatter(
            ortho_down[None].astype(jnp.bfloat16), "tensor", scatter_dimension=1, tiled=True
        ).astype(jnp.float32),
    )
    new_gate = apply_update(w_gate, piece_gate, gathered[4].shape)
    new_up = apply_update(w_up, piece_up, gathered[5].shape)
    new_down = apply_update(w_down, piece_down, gathered[6].shape)
    owner_list = [index * expert_count // 4 for index in range(4)]
    which_owned = jnp.zeros((), jnp.int32)
    for index in range(4):
        which_owned = jnp.where(expert_pos == owner_list[index], index + 1, which_owned)
    attn_branches = [solve_set(())] + [solve_set((index,)) for index in range(4)]
    attn_orthos = lax.switch(
        which_owned, attn_branches, (gathered[0], gathered[1], gathered[2], gathered[3])
    )
    attn_list = (
        (1, w_query.shape[1]),
        (1, w_key.shape[1]),
        (1, w_value.shape[1]),
        (0, w_out_proj.shape[0]),
    )
    pieces = []
    for matrix_index in range(4):
        along_dim, piece_width = attn_list[matrix_index]
        pieces.append(
            spread(
                shortened(
                    lax.dynamic_slice_in_dim(
                        attn_orthos[matrix_index], tensor_pos * piece_width, piece_width, along_dim
                    )
                ),
                "expert",
                owner_list[matrix_index],
            )
        )
    new_query = apply_update(expert_rows(w_query, 0), expert_rows(pieces[0], 0), gathered[0].shape)
    new_key = apply_update(expert_rows(w_key, 0), expert_rows(pieces[1], 0), gathered[1].shape)
    new_value = apply_update(expert_rows(w_value, 0), expert_rows(pieces[2], 0), gathered[2].shape)
    new_out_proj = apply_update(
        expert_rows(w_out_proj, 1), expert_rows(pieces[3], 1), gathered[3].shape
    )
    new_gain_attn = gain_attn - gain_rate * new_mom_gain_attn
    new_gain_ffn = gain_ffn - gain_rate * new_mom_gain_ffn
    return (
        block_out,
        grad_input,
        grad_query,
        grad_key,
        grad_value,
        grad_out_proj,
        grad_gate,
        grad_up,
        grad_down,
        grad_gain_attn,
        grad_gain_ffn,
        new_query,
        new_key,
        new_value,
        new_out_proj,
        new_gate,
        new_up,
        new_down,
        new_gain_attn,
        new_gain_ffn,
        new_mom_query,
        new_mom_key,
        new_mom_value,
        new_mom_out_proj,
        new_mom_gate,
        new_mom_up,
        new_mom_down,
        new_mom_gain_attn,
        new_mom_gain_ffn,
    )


def chip_index(z, y, x):
    return (z * 2 + y) * 2 + x


def chip_pairs(target):
    return [
        (chip_index(z, y, x), chip_index(*target(z, y, x)))
        for z in range(4)
        for y in range(2)
        for x in range(2)
    ]


FLIP_X = chip_pairs(lambda z, y, x: (z, y, 1 - x))
FLIP_Y = chip_pairs(lambda z, y, x: (z, 1 - y, x))
FLIP_Z1 = chip_pairs(lambda z, y, x: (z ^ 1, y, x))
FLIP_Z2 = chip_pairs(lambda z, y, x: (z ^ 2, y, x))
TURN_UP = [chip_pairs(lambda z, y, x, k=k: ((z + k) % 4, y, x)) for k in range(4)]
TURN_DOWN = [chip_pairs(lambda z, y, x, k=k: ((z - k) % 4, y, x)) for k in range(4)]


def across(value, pairs):
    return lax.ppermute(value, "expert", pairs)


def swap_core(value):
    return lax.ppermute(value, "tensor", [(0, 1), (1, 0)])


def matmul(left, right):
    return jnp.dot(left, right, preferred_element_type=jnp.float32)


def held(values, *others):
    return lax.optimization_barrier((values, others))[0]


def send_along_z(block):
    return [block] + [across(block, TURN_UP[k]) for k in range(1, 4)]


def first_hop(block):
    half = block.shape[0] // 2
    first, second = block[:half], block[half:]
    first_pair = jnp.concatenate([first, across(first, FLIP_X)])
    second_pair = jnp.concatenate([second, across(second, FLIP_Y)])
    return first_pair, second_pair


def second_hop(pairs):
    return pairs[0], across(pairs[0], FLIP_Y), pairs[1], across(pairs[1], FLIP_X)


def gather_weights(table):
    half = table.shape[1] // 2
    stack = jnp.stack([table] + [across(table, TURN_UP[k]) for k in range(1, 4)])
    with_x = jnp.stack([stack, across(stack, FLIP_X)])
    with_y = jnp.stack([with_x, across(with_x, FLIP_Y)])
    mine = lax.dynamic_index_in_dim(with_y, lax.axis_index("expert"), 3, keepdims=False)
    columns = []
    for k in range(4):
        first, second = mine[:, :, k, :half], mine[:, :, k, half:]
        order = [first[0, 0], first[0, 1], first[1, 0], first[1, 1]]
        order += [second[0, 0], second[1, 0], second[0, 1], second[1, 1]]
        columns.append(jnp.concatenate(order)[:, None])
    return columns


def add_low(left, right):
    return (left.astype(jnp.float32) + right.astype(jnp.float32)).astype(jnp.bfloat16)


def return_group(parts, k):
    half = parts[0].shape[0] // 2
    first = add_low(parts[0], across(parts[1], FLIP_Y))
    second = add_low(parts[2], across(parts[3], FLIP_X))
    first_sum = add_low(first[:half], across(first[half:], FLIP_X))
    second_sum = add_low(second[:half], across(second[half:], FLIP_Y))
    total = jnp.concatenate([first_sum, second_sum])
    return across(total, TURN_DOWN[k]) if k else total


PARTS = 4


def expert_kernel(carried, *refs):
    row_parts, top_parts = refs[:PARTS], refs[PARTS : 2 * PARTS]
    weight_ref, gate_ref, up_ref, down_ref, gate_t_ref, up_t_ref, down_t_ref = refs[
        2 * PARTS : 2 * PARTS + 7
    ]
    outs = refs[2 * PARTS + 7 + carried :]
    rows_ref, tops_ref, hidden_ref, act_grad_ref = outs[:4]
    input_parts, out_parts = outs[4 : 4 + PARTS], outs[4 + PARTS : 4 + 2 * PARTS]
    row_buf, top_buf, input_buf, out_buf, in_sem, out_sem = outs[4 + 2 * PARTS :]
    step = pl.program_id(0)
    slot = lax.rem(step, 2)

    def arrivals(part):
        at = part % 2
        return (
            pltpu.make_async_copy(row_parts[part], row_buf.at[at], in_sem.at[0, at]),
            pltpu.make_async_copy(top_parts[part], top_buf.at[at], in_sem.at[1, at]),
        )

    def departures(part):
        at = part % 2
        return (
            pltpu.make_async_copy(input_buf.at[at], input_parts[part], out_sem.at[0, at]),
            pltpu.make_async_copy(out_buf.at[at], out_parts[part], out_sem.at[1, at]),
        )

    def on_step(which, action):
        @pl.when(step == which)
        def _():
            action()

    def start(copies):
        for copy in copies:
            copy.start()

    def wait(copies):
        for copy in copies:
            copy.wait()

    on_step(0, lambda: start(arrivals(0)))
    for part in range(1, PARTS):
        on_step(part - 1, lambda part=part: start(arrivals(part)))
    for part in range(PARTS):
        on_step(part, lambda part=part: wait(arrivals(part)))
    for part in range(2, PARTS):
        on_step(part, lambda part=part: wait(departures(part - 2)))
    rows = row_buf[slot]
    tops = top_buf[slot]
    rows_ref[...] = rows
    tops_ref[...] = tops
    weight = weight_ref[...]
    width = hidden_ref.shape[1]
    gate = matmul(rows, gate_ref[...])
    up = matmul(rows, up_ref[...])
    grad_hidden = matmul(tops, down_t_ref[...]) * weight
    logistic = 1.0 / (1.0 + jnp.exp(-gate))
    activated = gate * logistic
    hidden_ref[...] = (activated * up * weight).astype(jnp.bfloat16)
    grad_gate = (grad_hidden * up * logistic * (1.0 + gate * (1.0 - logistic))).astype(jnp.bfloat16)
    grad_up = (grad_hidden * activated).astype(jnp.bfloat16)
    act_grad_ref[:, :width] = grad_gate
    act_grad_ref[:, width:] = grad_up
    input_buf[slot] = (matmul(grad_gate, gate_t_ref[...]) + matmul(grad_up, up_t_ref[...])).astype(
        jnp.bfloat16
    )
    out_buf[slot] = matmul(hidden_ref[...], down_ref[...]).astype(jnp.bfloat16)
    for part in range(PARTS):
        on_step(part, lambda part=part: start(departures(part)))
    for part in range(PARTS - 2, PARTS):
        on_step(PARTS - 1, lambda part=part: wait(departures(part)))


def expert_rows_call(group, row_parts, top_parts, weight, mats, carried):
    tile, width = row_parts[0].shape
    hidden = mats[0].shape[1]
    count = PARTS * tile
    anywhere = pl.BlockSpec(memory_space=pl.ANY)
    place = lambda columns: pl.BlockSpec((tile, columns), lambda i: (group * PARTS + i, 0))
    whole = lambda mat: pl.BlockSpec(mat.shape, lambda i: (0, 0), pipeline_mode=pl.Buffered(1))
    kept = [(4 * count, columns) for columns in (width, width, hidden, 2 * hidden)]
    low = lambda shape: jax.ShapeDtypeStruct(shape, jnp.bfloat16)
    first_carried = 2 * PARTS + 1 + len(mats)
    results = pl.pallas_call(
        functools.partial(expert_kernel, len(carried)),
        grid=(PARTS,),
        in_specs=[anywhere] * (2 * PARTS)
        + [pl.BlockSpec((tile, 1), lambda i: (i, 0))]
        + [whole(mat) for mat in mats]
        + [anywhere] * len(carried),
        out_specs=[place(shape[1]) for shape in kept] + [anywhere] * (2 * PARTS),
        out_shape=[low(shape) for shape in kept] + [low((tile, width))] * (2 * PARTS),
        input_output_aliases={first_carried + index: index for index in range(len(carried))},
        scratch_shapes=[pltpu.VMEM((2, tile, width), jnp.bfloat16)] * 4
        + [pltpu.SemaphoreType.DMA((2, 2))] * 2,
        compiler_params=pltpu.CompilerParams(vmem_limit_bytes=48 << 20),
        cost_estimate=pl.CostEstimate(
            flops=12 * count * width * hidden,
            bytes_accessed=2 * (6 * count * width + 3 * count * hidden + 6 * width * hidden),
            transcendentals=count * hidden,
        ),
        name="expert_rows",
    )(*row_parts, *top_parts, weight, *mats, *carried)
    return results[:4], results[4 : 4 + PARTS], results[4 + PARTS :]


def contract(left, right):
    return lax.dot_general(left, right, (((1,), (1,)), ((), ())), preferred_element_type=jnp.float32)


def newton_rounds(iterate_ref, gram_ref):
    rows = iterate_ref.shape[0]
    wide = iterate_ref[...].astype(jnp.float32)
    scale = 1.0 / (jnp.sqrt(jnp.sum(wide * wide)) + 1e-07)
    iterate_ref[...] = (wide * scale).astype(jnp.bfloat16)
    for _ in range(NS_ITERS):
        gram_ref[...] = contract(iterate_ref[...], iterate_ref[...]).astype(jnp.bfloat16)
        gram = gram_ref[...]
        square = matmul(gram, gram)
        poly = (coeff_two * gram.astype(jnp.float32) + coeff_three * square).astype(jnp.bfloat16)
        iterate = iterate_ref[...]
        iterate_ref[...] = (
            coeff_one * iterate.astype(jnp.float32) + matmul(poly, iterate)
        ).astype(jnp.bfloat16)


def flipped(value):
    return value.astype(jnp.float32).T.astype(jnp.bfloat16)


def tall_solve_kernel(first_ref, second_ref, first_out_ref, second_out_ref, iterate_ref, gram_ref):
    half = first_ref.shape[1]
    iterate_ref[:half] = flipped(first_ref[...])
    iterate_ref[half:] = flipped(second_ref[...])
    newton_rounds(iterate_ref, gram_ref)
    first_out_ref[...] = flipped(iterate_ref[:half])
    second_out_ref[...] = flipped(iterate_ref[half:])


def wide_solve_kernel(first_ref, second_ref, first_out_ref, iterate_ref, gram_ref):
    half = first_ref.shape[0]
    iterate_ref[:half] = first_ref[...]
    iterate_ref[half:] = second_ref[...]
    newton_rounds(iterate_ref, gram_ref)
    first_out_ref[...] = iterate_ref[:half]


def half_solve(first, second, tall):
    half, columns = min(first.shape), max(first.shape)
    rows = 2 * half
    results = 2 if tall else 1
    return pl.pallas_call(
        tall_solve_kernel if tall else wide_solve_kernel,
        out_shape=[jax.ShapeDtypeStruct(first.shape, jnp.bfloat16)] * results,
        in_specs=[pl.BlockSpec(memory_space=pltpu.VMEM)] * 2,
        out_specs=[pl.BlockSpec(memory_space=pltpu.VMEM)] * results,
        scratch_shapes=[
            pltpu.VMEM((rows, columns), jnp.bfloat16),
            pltpu.VMEM((rows, rows), jnp.bfloat16),
        ],
        compiler_params=pltpu.CompilerParams(vmem_limit_bytes=40 << 20),
        cost_estimate=pl.CostEstimate(
            flops=NS_ITERS * 2 * rows * rows * (2 * columns + rows),
            bytes_accessed=2 * rows * columns * (1 + results),
            transcendentals=0,
        ),
        name="tall_solve" if tall else "wide_solve",
    )(first, second)


def large_solve_kernel(
    first_start_ref, first_ref, second_ref, out_ref, matrix, gram, mix, gram_next, other
):
    size = matrix.shape[0]
    half = first_ref.shape[0]
    tile = 256
    count = out_ref.shape[1]
    matrix[:half] = first_ref[...]
    matrix[half:] = second_ref[...]

    def add_square(i, total):
        wide = matrix[pl.ds(pl.multiple_of(i * tile, tile), tile)].astype(jnp.float32)
        return total + jnp.sum(wide * wide)

    total = lax.fori_loop(0, size // tile, add_square, jnp.float32(0.0))
    scale = 1.0 / (jnp.sqrt(total) + 1e-07)

    def by_rows(target, value_of):
        @pl.loop(0, size // tile)
        def _(i):
            at = pl.ds(pl.multiple_of(i * tile, tile), tile)
            target[at] = value_of(at).astype(jnp.bfloat16)

    def poly(source):
        return lambda at: (
            coeff_two * source[at].astype(jnp.float32)
            + coeff_three * matmul(source[at], source[...])
        )

    by_rows(gram, lambda at: contract(matrix[at], matrix[...]) * (scale * scale))
    by_rows(mix, poly(gram))
    by_rows(other, lambda at: coeff_one * gram[at].astype(jnp.float32) + matmul(mix[at], gram[...]))
    by_rows(gram_next, lambda at: coeff_one * other[at].astype(jnp.float32) + matmul(other[at], mix[...]))

    row_ids = lax.broadcasted_iota(jnp.int32, (size, count), 0)
    column_ids = lax.broadcasted_iota(jnp.int32, (size, count), 1)
    picked = jnp.where(row_ids == column_ids + first_start_ref[0], 1.0, 0.0).astype(jnp.bfloat16)
    columns = matmul(matrix[...], picked) * scale
    columns = coeff_one * columns + matmul(mix[...], columns.astype(jnp.bfloat16))
    by_rows(other, poly(gram_next))

    def second_poly(value):
        return coeff_one * value + matmul(other[...], value.astype(jnp.bfloat16))

    def last_gram(value):
        return second_poly(matmul(gram_next[...], second_poly(value).astype(jnp.bfloat16)))

    columns = second_poly(columns)
    once = last_gram(columns)
    twice = last_gram(once)
    out_ref[...] = (coeff_one * columns + coeff_two * once + coeff_three * twice).astype(jnp.bfloat16)


def large_solve(first, second, start, count):
    half, size = first.shape
    vmem = pl.BlockSpec(memory_space=pltpu.VMEM)
    return pl.pallas_call(
        large_solve_kernel,
        out_shape=jax.ShapeDtypeStruct((size, count), jnp.bfloat16),
        in_specs=[pl.BlockSpec(memory_space=pltpu.SMEM), vmem, vmem],
        out_specs=vmem,
        scratch_shapes=[pltpu.VMEM((size, size), jnp.bfloat16)] * 5,
        compiler_params=pltpu.CompilerParams(vmem_limit_bytes=56 << 20),
        cost_estimate=pl.CostEstimate(
            flops=2 * size * size * (5 * size + 8 * count),
            bytes_accessed=2 * size * size,
            transcendentals=0,
        ),
        name="large_solve",
    )(start, first, second)


def chip_place():
    chip = lax.axis_index("expert")
    return chip // 4, chip // 2 % 2, chip % 2


def sum_shards(first, second):
    z, y, x = chip_place()
    rows, columns = first.shape[0] // 16, first.shape[1]

    def halve(value, axis, at, pairs):
        keep = lax.dynamic_index_in_dim(value, at, axis, keepdims=False)
        send = lax.dynamic_index_in_dim(value, 1 - at, axis, keepdims=False)
        return add_low(keep, across(send, pairs))

    first = halve(first.reshape(4, 2, 2, rows, columns), 1, y, FLIP_Y)
    second = halve(second.reshape(4, 2, 2, rows, columns), 2, x, FLIP_X)
    cut = jnp.stack([halve(first, 1, x, FLIP_X), halve(second, 1, y, FLIP_Y)], axis=1)
    total = lax.dynamic_index_in_dim(cut, z, 0, keepdims=False).astype(jnp.float32)
    for k in range(1, 4):
        send = lax.dynamic_index_in_dim(cut, (z + 4 - k) % 4, 0, keepdims=False)
        total = total + across(send, TURN_DOWN[k]).astype(jnp.float32)
    return total.astype(jnp.bfloat16)


def join_shards(shard):
    z, y, x = chip_place()
    columns = shard.shape[2]
    moved = [shard] + [across(shard, TURN_UP[k]) for k in range(1, 4)]
    turn = [moved[0], moved[3], moved[2], moved[1]]
    stack = lax.dynamic_slice_in_dim(jnp.stack(turn + turn[:3]), (4 - z) % 4, 4, 0)

    def double(value, axis, at, pairs):
        other = across(value, pairs)
        return jnp.where(at == 0, jnp.stack([value, other], axis), jnp.stack([other, value], axis))

    first = double(double(stack[:, 0], 1, x, FLIP_X), 1, y, FLIP_Y)
    second = double(double(stack[:, 1], 1, y, FLIP_Y), 2, x, FLIP_X)
    return first.reshape(-1, columns), second.reshape(-1, columns)


def sum_everywhere(value):
    value = value + swap_core(value)
    for pairs in (FLIP_X, FLIP_Y, FLIP_Z1, FLIP_Z2):
        value = value + across(value, pairs)
    return value


def own_half(value, axis=0):
    size = value.shape[axis] // 2
    return lax.dynamic_slice_in_dim(value, lax.axis_index("tensor") * size, size, axis)


def other_half(value, axis=0):
    size = value.shape[axis] // 2
    return lax.dynamic_slice_in_dim(value, (1 - lax.axis_index("tensor")) * size, size, axis)


def both_halves(value):
    other = swap_core(value)
    first = lax.axis_index("tensor") == 0
    return jnp.concatenate([jnp.where(first, value, other), jnp.where(first, other, value)])


def per_core(
    block_in,
    segments,
    routes,
    route_weights,
    gain_attn,
    gain_ffn,
    w_query,
    w_key,
    w_value,
    w_out_proj,
    w_gate,
    w_up,
    w_down,
    mom_query,
    mom_key,
    mom_value,
    mom_out_proj,
    mom_gate,
    mom_up,
    mom_down,
    mom_gain_attn,
    mom_gain_ffn,
    cotangent,
):
    tok_rows, width = block_in.shape
    experts = lax.axis_size("expert")
    tensor_pos = lax.axis_index("tensor")
    expert_pos = lax.axis_index("expert")
    first_core = tensor_pos == 0

    own_top = own_half(cotangent)
    tops_z = send_along_z(own_top)
    top_pairs = [first_hop(tops_z[0])]
    own_routes = own_half(routes)
    own_scales = own_half(route_weights)
    named = own_routes[None] == jnp.arange(experts, dtype=jnp.int32)[:, None, None]
    table = jnp.sum(jnp.where(named, own_scales[None], 0.0), axis=2)

    residual_in = block_in.astype(jnp.float32)
    inv_first = lax.rsqrt(jnp.mean(residual_in * residual_in, axis=1, keepdims=True) + norm_eps)
    normed_attn = (residual_in * inv_first * gain_attn).astype(jnp.bfloat16)
    queries = (matmul(normed_attn, w_query) * HD ** (-0.5)).astype(jnp.bfloat16)
    key_rows = matmul(normed_attn, w_key).astype(jnp.bfloat16)
    value_rows = matmul(normed_attn, w_value).astype(jnp.bfloat16)
    queries, key_rows, value_rows = held((queries, key_rows, value_rows), top_pairs[0])
    top_parts = [second_hop(top_pairs[0])]
    log_total, attn_mixed = attend_forward((queries, key_rows, value_rows, segments))
    attn_mixed = held(attn_mixed, tops_z[1])
    top_pairs.append(first_hop(tops_z[1]))
    attn_part = matmul(attn_mixed, w_out_proj)
    own_in = own_half(residual_in)
    attn_other = swap_core(other_half(attn_part).astype(jnp.bfloat16))
    hidden_state = own_in + own_half(attn_part) + attn_other.astype(jnp.float32)
    inv_second = lax.rsqrt(jnp.mean(hidden_state * hidden_state, axis=1, keepdims=True) + norm_eps)
    normed_ffn = (hidden_state * inv_second * gain_ffn).astype(jnp.bfloat16)
    normed_ffn = held(normed_ffn, top_pairs[1], tops_z[2])
    top_parts.append(second_hop(top_pairs[1]))
    top_pairs.append(first_hop(tops_z[2]))
    rows_z = send_along_z(normed_ffn)

    w_gate_own, w_up_own, w_down_own, table = held((w_gate[0], w_up[0], w_down[0], table), normed_ffn)
    half = w_gate.shape[2]
    ff = 2 * half
    gate_mat = jnp.concatenate([w_gate_own, swap_core(w_gate_own)], axis=1)
    up_mat = jnp.concatenate([w_up_own, swap_core(w_up_own)], axis=1)
    down_mat = jnp.concatenate([w_down_own, swap_core(w_down_own)], axis=0)
    columns = gather_weights(table)
    mats = (gate_mat, up_mat, down_mat, gate_mat.T, up_mat.T, down_mat.T)
    mats = held(mats, top_pairs[2], tops_z[3])
    top_parts.append(second_hop(top_pairs[2]))
    top_pairs.append(first_hop(tops_z[3]))
    top_parts.append(second_hop(top_pairs[3]))

    row_pairs = [first_hop(held(rows_z[0], top_pairs[3]))]
    row_pairs.append(first_hop(rows_z[1]))
    row_parts = [second_hop(row_pairs[0])]
    back_parts, out_parts, carried = [], [], ()
    for k in range(4):
        mine = row_parts[k]
        if k < 3:
            row_parts.append(second_hop(row_pairs[k + 1]))
            if k < 2:
                row_pairs.append(first_hop(rows_z[k + 2]))
                mine = held(mine, row_pairs[k + 1], rows_z[k + 2])
            else:
                mine = held(mine, row_pairs[k + 1])
        carried, input_parts, outs = expert_rows_call(k, mine, top_parts[k], columns[k], mats, carried)
        back_parts.append(return_group(input_parts, k))
        out_parts.append(outs)
    rows_all, tops_all, hidden_all, act_grads = carried
    grad_normed_ffn = sum(part.astype(jnp.float32) for part in back_parts)
    late_outs = held(out_parts[2:], grad_normed_ffn)
    moe_late = [return_group(late_outs[k - 2], k) for k in (3, 2)]

    over_rows = lambda left, right: lax.dot_general(
        left, right, (((0,), (0,)), ((), ())), preferred_element_type=jnp.float32
    )
    grad_pair = over_rows(rows_all, act_grads)
    grad_down_all = over_rows(hidden_all, tops_all)
    send_gate = grad_pair[:, half:ff].astype(jnp.bfloat16)
    send_up = grad_pair[:, ff + half :].astype(jnp.bfloat16)
    send_down = grad_down_all[half:].astype(jnp.bfloat16)
    grad_gate = grad_pair[:, :half] + swap_core(send_gate).astype(jnp.float32)
    grad_up = grad_pair[:, ff : ff + half] + swap_core(send_up).astype(jnp.float32)
    grad_down = grad_down_all[:half] + swap_core(send_down).astype(jnp.float32)
    new_mom_gate = momentum_decay * mom_gate + grad_gate[None]
    new_mom_up = momentum_decay * mom_up + grad_up[None]
    new_mom_down = momentum_decay * mom_down + grad_down[None]
    gate_low = new_mom_gate[0].astype(jnp.bfloat16)
    up_low = new_mom_up[0].astype(jnp.bfloat16)
    down_low = new_mom_down[0].astype(jnp.bfloat16)
    keep_low = jnp.where(first_core, gate_low, up_low)
    got_low = swap_core(jnp.where(first_core, up_low, gate_low))
    own_ortho, other_ortho = half_solve(keep_low, got_low, True)
    got_ortho = swap_core(other_ortho)
    ortho_gate = jnp.where(first_core, own_ortho, got_ortho)
    ortho_up = jnp.where(first_core, got_ortho, own_ortho)
    (ortho_down,) = half_solve(down_low, swap_core(down_low), False)

    def apply_update(weight, ortho_piece, larger):
        factor = learn_rate * 0.2 * math.sqrt(larger)
        return weight.astype(jnp.float32) - factor * ortho_piece.astype(jnp.float32)

    new_gate = apply_update(w_gate, ortho_gate[None], max(width, ff))
    new_up = apply_update(w_up, ortho_up[None], max(width, ff))
    new_down = apply_update(w_down, ortho_down[None], max(width, ff))

    gain_ffn_part = jnp.sum(grad_normed_ffn * hidden_state * inv_second, axis=0)
    scaled = grad_normed_ffn * gain_ffn
    grad_state = own_top.astype(jnp.float32) + inv_second * (
        scaled
        - hidden_state
        * inv_second
        * inv_second
        * jnp.mean(scaled * hidden_state, axis=1, keepdims=True)
    )
    grad_state_low = both_halves(grad_state.astype(jnp.bfloat16))
    grad_out_local = over_rows(attn_mixed, grad_state_low).astype(jnp.bfloat16)
    middle = grad_out_local.shape[1] // 2
    out_sums = sum_shards(grad_out_local[:, :middle], grad_out_local[:, middle:])
    grad_mixed = contract(grad_state_low, w_out_proj).astype(jnp.bfloat16)
    grad_queries, grad_keys, grad_values = attend_backward(
        (queries, key_rows, value_rows, segments, log_total, attn_mixed, grad_mixed)
    )
    query_cols = w_query.shape[1]
    grad_query_local = over_rows(normed_attn, grad_queries).astype(jnp.bfloat16)
    grad_key_local = over_rows(normed_attn, grad_keys).astype(jnp.bfloat16)
    grad_value_local = over_rows(normed_attn, grad_values).astype(jnp.bfloat16)
    query_sums = sum_shards(grad_query_local[:, : query_cols // 2], grad_query_local[:, query_cols // 2 :])
    pair_sums = sum_shards(*held((grad_key_local, grad_value_local), query_sums))
    grad_out_low = jnp.concatenate(join_shards(out_sums), axis=1)
    grad_query_low = jnp.concatenate(join_shards(query_sums), axis=1)
    grad_key_low, grad_value_low = join_shards(pair_sums)
    early_outs = held(out_parts[:2], grad_query_low)
    moe_sum = sum(part.astype(jnp.float32) for part in moe_late) + sum(
        return_group(early_outs[k], k).astype(jnp.float32) for k in (1, 0)
    )
    block_out = both_halves((hidden_state + moe_sum).astype(jnp.bfloat16))

    attn_input_part = (
        contract(grad_queries, w_query) + contract(grad_keys, w_key) + contract(grad_values, w_value)
    )
    attn_input_other = swap_core(other_half(attn_input_part).astype(jnp.bfloat16))
    grad_normed_attn = own_half(attn_input_part) + attn_input_other.astype(jnp.float32)
    own_inv = own_half(inv_first)
    gain_attn_part = jnp.sum(grad_normed_attn * own_in * own_inv, axis=0)
    scaled_first = grad_normed_attn * gain_attn
    grad_input = both_halves(
        grad_state
        + own_inv
        * (
            scaled_first
            - own_in
            * own_inv
            * own_inv
            * jnp.mean(scaled_first * own_in, axis=1, keepdims=True)
        )
    )
    gain_parts = held(jnp.stack([gain_attn_part, gain_ffn_part]), grad_query_low)
    gain_sums = sum_everywhere(gain_parts)
    grad_gain_attn, grad_gain_ffn = gain_sums[0], gain_sums[1]

    grad_query = grad_query_low.astype(jnp.float32)
    grad_key = grad_key_low.astype(jnp.float32)
    grad_out_proj = grad_out_low.astype(jnp.float32)
    grad_value = grad_value_low.astype(jnp.float32)
    new_mom_query = momentum_decay * mom_query + grad_query
    new_mom_key = momentum_decay * mom_key + grad_key
    new_mom_value = momentum_decay * mom_value + grad_value
    new_mom_out_proj = momentum_decay * mom_out_proj + grad_out_proj
    new_mom_gain_attn = momentum_decay * mom_gain_attn + grad_gain_attn
    new_mom_gain_ffn = momentum_decay * mom_gain_ffn + grad_gain_ffn

    rows_first = Layout(major_to_minor=(0, 1))
    query_rows = with_layout_constraint(new_mom_query.astype(jnp.bfloat16), rows_first).T
    out_proj_rows = new_mom_out_proj.astype(jnp.bfloat16)
    large_keep = jnp.where(first_core, query_rows, out_proj_rows)
    large_send = jnp.where(first_core, out_proj_rows, query_rows)
    piece = width // experts
    large_cols = large_solve(
        large_keep, swap_core(large_send), (expert_pos * piece)[None], -(-piece // 128) * 128
    )[:, :piece]
    out_rows_count = w_out_proj.shape[0]
    got_large = swap_core(large_cols[out_rows_count:])
    query_piece = jnp.where(first_core, large_cols[:out_rows_count], got_large).T
    out_piece = jnp.where(first_core, got_large, large_cols[:out_rows_count])

    def expert_rows(matrix, along_dim):
        return lax.dynamic_slice_in_dim(matrix, expert_pos * piece, piece, along_dim)

    key_low = new_mom_key.astype(jnp.bfloat16)
    value_low = new_mom_value.astype(jnp.bfloat16)
    small_got = swap_core(jnp.where(first_core, value_low, key_low))
    own_small, other_small = half_solve(jnp.where(first_core, key_low, value_low), small_got, True)
    own_small = expert_rows(own_small, 0)
    got_small = swap_core(expert_rows(other_small, 0))
    key_piece = jnp.where(first_core, own_small, got_small)
    value_piece = jnp.where(first_core, got_small, own_small)

    new_query = apply_update(expert_rows(w_query, 0), query_piece, width)
    new_key = apply_update(expert_rows(w_key, 0), key_piece, width)
    new_value = apply_update(expert_rows(w_value, 0), value_piece, width)
    new_out_proj = apply_update(expert_rows(w_out_proj, 1), out_piece, width)
    new_gain_attn = gain_attn - gain_rate * new_mom_gain_attn
    new_gain_ffn = gain_ffn - gain_rate * new_mom_gain_ffn
    return (
        block_out,
        grad_input,
        grad_query,
        grad_key,
        grad_value,
        grad_out_proj,
        grad_gate[None],
        grad_up[None],
        grad_down[None],
        grad_gain_attn,
        grad_gain_ffn,
        new_query,
        new_key,
        new_value,
        new_out_proj,
        new_gate,
        new_up,
        new_down,
        new_gain_attn,
        new_gain_ffn,
        new_mom_query,
        new_mom_key,
        new_mom_value,
        new_mom_out_proj,
        new_mom_gate,
        new_mom_up,
        new_mom_down,
        new_mom_gain_attn,
        new_mom_gain_ffn,
    )


def solution(mesh):
    placed = (
        P("expert", None),
        P("expert"),
        P("expert", None),
        P("expert", None),
        P(),
        P(),
        P(None, "tensor"),
        P(None, "tensor"),
        P(None, "tensor"),
        P("tensor", None),
        P("expert", None, "tensor"),
        P("expert", None, "tensor"),
        P("expert", "tensor", None),
        P(None, "tensor"),
        P(None, "tensor"),
        P(None, "tensor"),
        P("tensor", None),
        P("expert", None, "tensor"),
        P("expert", None, "tensor"),
        P("expert", "tensor", None),
        P(),
        P(),
        P("expert", None),
    )
    blocked = mesh.shape["expert"] == 16 and mesh.shape["tensor"] == 2
    return jax.shard_map(
        per_core if blocked else per_device,
        mesh=mesh,
        in_specs=placed,
        out_specs=(
            P("expert", None),
            P("expert", None),
            P(None, "tensor"),
            P(None, "tensor"),
            P(None, "tensor"),
            P("tensor", None),
            P("expert", None, "tensor"),
            P("expert", None, "tensor"),
            P("expert", "tensor", None),
            P(),
            P(),
            P("expert", "tensor"),
            P("expert", "tensor"),
            P("expert", "tensor"),
            P("tensor", "expert"),
            P("expert", None, "tensor"),
            P("expert", None, "tensor"),
            P("expert", "tensor", None),
            P(),
            P(),
            P(None, "tensor"),
            P(None, "tensor"),
            P(None, "tensor"),
            P("tensor", None),
            P("expert", None, "tensor"),
            P("expert", None, "tensor"),
            P("expert", "tensor", None),
            P(),
            P(),
        ),
        check_vma=False,
    )
```
